256 devices in a mesh: bunch: 64 (over z, y_lo, x), dom: 4 (over y_hi, core).
Axes of the slice: x: 4, y: 4 (y_hi: 2, y_lo: 2; y = y_hi * 2 + y_lo), z: 8, core: 2. Of those that a mesh axis runs over, the one named last changes fastest.
Arguments:
- positions: float32 [2, 2, 128, 4096], P(None, None, 'bunch', 'dom'), may hold values from 0 to 127
- momenta: float32 [2, 2, 128, 4096], P(None, None, 'bunch', 'dom'), may hold values from -6 to 6
- kernel_hat: float32 [2, 2, 256, 256], replicated, may hold values from -1.2 to 1.2
- partners: int32 [2, 128, 16], P(None, 'bunch'), may hold values from 0 to 127, as said below
- offsets: int32 [2, 2, 128, 16], P(None, None, 'bunch'), may hold values from -32 to 32
- counts: int32 [2, 128], P(None, 'bunch'), may hold values from 1 to 16, as said below
Outputs:
- kicked: float32 [2, 2, 128, 4096], P(None, None, 'bunch', 'dom')
The draws below stay inside these ranges and needn't reach their ends.
Inputs may be any that keep to these rules, and one draw needn't show every extreme that they name: partners[e, b, s] // 2 lies at most 2 from b // 2, counted around a cycle of 64 blocks. `counts`: the first bunch of each block of 2 bunches has all 16 slots live.
All inputs are finite; a program needn't handle non-finite values.
Results may differ from the reference program's by a relative error of at most 0.0003.
Values sent between devices are 32-bit elements; how exact they have to be, the bound alone decides.
No kernel may reach another device: no remote copies, remote signals or barrier semaphores. Data moves between devices by JAX's collectives and lax.ppermute only.
A program may use at most 64 MiB of HBM per device.

```python
import jax
import jax.numpy as jnp
from jax import lax

GRID = 128
PAD = 256
BPB = 2
SLOTS = 16
HOPS = 2
OFFSET = 32
NB = 128
PART = 4096


def draw_partners(key, part):
    key_block = jax.random.fold_in(key, 11)
    key_member = jax.random.fold_in(key, 12)
    blocks = NB // BPB
    home = (jnp.arange(NB, dtype=jnp.int32) // BPB)[None, :, None]
    jumps = jax.random.randint(key_block, (2, NB, SLOTS), 0 - HOPS, HOPS + 1)
    member = jax.random.randint(key_member, (2, NB, SLOTS), 0, BPB)
    return ((home + jumps) % blocks * BPB + member).astype(jnp.int32)


def draw_counts(key, part):
    key_count = jax.random.fold_in(key, 21)
    drawn = jax.random.randint(key_count, (2, NB), 1, SLOTS + 1)
    first = (jnp.arange(NB, dtype=jnp.int32) % BPB == 0)[None, :]
    return jnp.where(first, SLOTS, drawn).astype(jnp.int32)


def touch_ends(array, key, low, largest):
    dims = array.shape
    place = [jax.random.randint(jax.random.fold_in(key, axis), (), 0, dims[axis]) for axis in range(len(dims))]
    array = array.at[tuple(place)].set(low)
    longest = dims.index(max(dims))
    place[longest] = (place[longest] + 1) % dims[longest]
    return array.at[tuple(place)].set(largest)


def levels(stream_key, extent, cuts, low, high):
    gain = 1.0
    for dim, parts in cuts:
        steps = jax.random.uniform(jax.random.fold_in(jax.random.fold_in(stream_key, 6), dim), (parts,), jnp.float32, low / len(cuts), high / len(cuts))
        gain = gain * jnp.repeat(jnp.exp(steps), extent[dim] // parts).reshape((-1,) + (1,) * (len(extent) - 1 - dim))
    return gain


def centred(key, dims, deviation, reach, pieces=(), kind=jnp.bfloat16):
    entries = deviation * jax.random.normal(key, dims, jnp.float32)
    if pieces:
        entries = entries * levels(key, dims, pieces, -0.22, 0.18)
    return jnp.clip(entries, -reach, reach).astype(kind)


def setup_inputs(seed: int = 0) -> dict:
    arg_keys = jax.random.split(jax.random.key(seed), 7)
    positions = jnp.clip(127.0 * jax.random.uniform(arg_keys[0], (2, 2, NB, PART), jnp.float32) ** levels(arg_keys[0], (2, 2, NB, PART), ((2, 64), (3, 4)), -0.2, 0.2), 0.0, 127.0)
    momenta = centred(arg_keys[1], (2, 2, NB, PART), 1.0, 6.0, ((2, 64), (3, 4)), jnp.float32)
    kernel_hat = centred(arg_keys[2], (2, 2, PAD, PAD), 0.2, 1.2, (), jnp.float32)
    partners = draw_partners(jax.random.fold_in(arg_keys[6], 71), 0)
    offsets = touch_ends(jax.random.randint(arg_keys[4], (2, 2, NB, SLOTS), 0 - OFFSET, OFFSET + 1), jax.random.fold_in(arg_keys[4], 1), 0 - OFFSET, OFFSET).astype(jnp.int32)
    counts = draw_counts(jax.random.fold_in(arg_keys[6], 71), 0)
    return dict(positions=positions, momenta=momenta, kernel_hat=kernel_hat, partners=partners, offsets=offsets, counts=counts)


HIGH = lax.Precision.HIGHEST


def hat_table(coord):
    cells = jnp.arange(GRID, dtype=jnp.float32)
    return jnp.maximum(0.0, 1.0 - jnp.abs(coord[:, None] - cells[None, :]))


def deposit(coords):
    weight_x = hat_table(coords[0])
    weight_y = hat_table(coords[1])
    return jnp.dot(weight_x.T, weight_y, precision=HIGH, preferred_element_type=jnp.float32)


def kick(coords, fields, moments):
    weight_x = hat_table(coords[0])
    weight_y = hat_table(coords[1])
    field_x = jnp.sum(jnp.dot(weight_x, fields[0], precision=HIGH, preferred_element_type=jnp.float32) * weight_y, axis=1)
    field_y = jnp.sum(jnp.dot(weight_x, fields[1], precision=HIGH, preferred_element_type=jnp.float32) * weight_y, axis=1)
    return moments + jnp.stack([field_x, field_y])


def reference(positions, momenta, kernel_hat, partners, offsets, counts):
    coords = jnp.transpose(positions.reshape(2, 2 * NB, PART), (1, 0, 2))
    grids = lax.map(deposit, coords)

    def field_of(target):
        beam = target // NB
        bunch = target % NB
        row = partners[beam, bunch]
        shift_x = offsets[0, beam, bunch]
        shift_y = offsets[1, beam, bunch]
        live_count = counts[beam, bunch]

        def add_one(slot, total):
            index = ((1 - beam) * NB + row[slot]).astype(jnp.int32)
            grid = lax.dynamic_index_in_dim(grids, index, 0, keepdims=False)
            padded = jnp.pad(grid, ((0, PAD - GRID), (0, PAD - GRID)))
            moved = jnp.roll(padded, (shift_x[slot], shift_y[slot]), axis=(0, 1))
            live = (slot < live_count).astype(jnp.float32)
            return total + live * moved

        summed = lax.fori_loop(0, SLOTS, add_one, jnp.zeros((PAD, PAD), jnp.float32))
        spectrum = jnp.fft.fft2(summed)
        kernel = kernel_hat[:, 0] + 1j * kernel_hat[:, 1]
        return jnp.real(jnp.fft.ifft2(kernel * spectrum[None]))[:, :GRID, :GRID]

    fields = lax.map(field_of, jnp.arange(2 * NB, dtype=jnp.int32))
    moments = jnp.transpose(momenta.reshape(2, 2 * NB, PART), (1, 0, 2))
    kicked = lax.map(lambda item: kick(item[0], item[1], item[2]), (coords, fields, moments))
    return jnp.transpose(kicked, (1, 0, 2)).reshape(2, 2, NB, PART)
```

```python
import jax
import jax.numpy as jnp
import numpy as np
from jax import lax
from jax.experimental import pallas as pl
from jax.experimental.pallas import tpu as pltpu
from jax.sharding import PartitionSpec as P

GRID = 128
PAD = 256
OFFSET = 32
SPAN = GRID + 2 * OFFSET
BF = jnp.bfloat16
F32 = jnp.float32


def split_const(m):
    hi = m.astype(BF)
    lo = (m - hi.astype(np.float64)).astype(BF)
    return np.asarray(hi), np.asarray(lo)


def dft_tables():
    k = np.arange(PAD)
    w = 2.0 * np.pi / PAD
    r = np.arange(SPAN) - OFFSET
    ang = w * ((k[:, None] * r[None, :]) % PAD)
    hi, lo = split_const(np.concatenate([np.cos(ang), -np.sin(ang)], 0))
    rows = np.concatenate([hi, hi, lo], 1)
    r = np.arange(PAD) - OFFSET
    ang = w * ((r[:, None] * k[None, :]) % PAD)
    hi, lo = split_const(np.concatenate([np.cos(ang), np.sin(ang)], 1))
    cols = np.concatenate([hi, hi, lo], 0)
    j = np.arange(GRID)
    ang = w * ((k[:, None] * j[None, :]) % PAD)
    hi, lo = split_const(np.concatenate([np.cos(ang), np.sin(ang)], 1))
    back_cols = np.concatenate([hi, hi, lo], 0)
    ang = ang.T
    hi, lo = split_const(np.concatenate([np.cos(ang), -np.sin(ang)], 1) / (PAD * PAD))
    back_rows = np.concatenate([hi, hi, lo], 1)
    return rows, cols, back_cols, back_rows


def hilo(v):
    hi = v.astype(BF)
    lo = (v - hi.astype(F32)).astype(BF)
    return hi, lo


def dot(a, b):
    return jnp.dot(a, b, preferred_element_type=F32)


def hat(coord, lanes):
    cells = lax.broadcasted_iota(jnp.int32, (GRID, lanes), 0).astype(F32)
    return jnp.maximum(0.0, 1.0 - jnp.abs(coord - cells))


def deposit_body(where_ref, a_ref, b_ref, *rest):
    if len(rest) == 4:
        prev_ref, out_ref, tx, ty = rest
    else:
        prev_ref = None
        out_ref, tx, ty = rest
    e = 1 - where_ref[1]
    n = a_ref.shape[-1]
    for m in range(2):
        for i, ref in enumerate((a_ref, b_ref)):
            for coord, table in ((0, tx), (1, ty)):
                hi, lo = hilo(hat(ref[coord, e, pl.ds(m, 1), :], n))
                table[m, 0:GRID, i * n : (i + 1) * n] = hi
                table[m, GRID:, i * n : (i + 1) * n] = lo
        acc = lax.dot_general(
            tx[m], ty[m], (((1,), (1,)), ((), ())), preferred_element_type=F32
        )
        total = (acc[:GRID, :GRID] + acc[GRID:, GRID:]) + (acc[:GRID, GRID:] + acc[GRID:, :GRID])
        if prev_ref is not None:
            total = total + prev_ref[m]
        out_ref[m] = total


def deposit(where, a, b, prev=None):
    n = a.shape[-1]
    vm = pl.BlockSpec(memory_space=pltpu.VMEM)
    args = [where, a, b] + ([] if prev is None else [prev])
    return pl.pallas_call(
        deposit_body,
        out_shape=jax.ShapeDtypeStruct((2, GRID, GRID), F32),
        in_specs=[pl.BlockSpec(memory_space=pltpu.SMEM)] + [vm] * (len(args) - 1),
        out_specs=vm,
        scratch_shapes=[pltpu.VMEM((2, 2 * GRID, 2 * n), BF)] * 2,
        compiler_params=pltpu.CompilerParams(vmem_limit_bytes=16 * 1024 * 1024),
        name="deposit_first" if prev is None else "deposit_second",
    )(*args)


def field_body(
    where_ref, partners_ref, offsets_ref, counts_ref,
    own_ref, r1_ref, r2_ref, s1_ref, s2_ref,
    kernel_hbm, rows_hbm, cols_hbm, bcols_hbm, brows_hbm,
    pa_ref, pc_ref, py_ref, pyc_ref,
    near_ref, far_ref,
    grids, source, rows_ref, cols_ref, kern, bcols_ref, brows_ref, gsem, ksem,
):
    b = where_ref[0]
    h = where_ref[1]
    c = where_ref[2]
    ndev = where_ref[3]
    places = (2, 1 + 2 * c, 4 * c, 3 - 2 * c, 4 - 4 * c)
    copies = [
        pltpu.make_async_copy(ref, grids.at[place], gsem.at[i])
        for i, (ref, place) in enumerate(zip((own_ref, r1_ref, r2_ref, s1_ref, s2_ref), places))
    ]
    fixed = [
        pltpu.make_async_copy(src, dst, ksem.at[i])
        for i, (src, dst) in enumerate((
            (rows_hbm, rows_ref), (cols_hbm, cols_ref), (kernel_hbm, kern),
            (bcols_hbm, bcols_ref), (brows_hbm, brows_ref),
        ))
    ]
    for copy in copies + fixed:
        copy.start()
    source[...] = jnp.zeros_like(source)
    lane = lax.broadcasted_iota(jnp.int32, (GRID, GRID), 1)
    for copy in copies:
        copy.wait()

    def add_slot(s, carry):
        p = partners_ref[h, c, s]
        rel = lax.rem(p // 2 - b + 2 + 2 * ndev, ndev)
        r0 = offsets_ref[0, h, c, s] + OFFSET
        c0 = offsets_ref[1, h, c, s] + OFFSET
        grid = grids[rel, p % 2]
        turned = pltpu.roll(grid, c0, 1)
        low = jnp.where(lane >= c0, turned, 0.0)
        high = jnp.where(lane >= c0, 0.0, turned)
        source[0, pl.ds(r0, GRID), :] += low
        source[1, pl.ds(r0, GRID), :] += high
        return carry

    lax.fori_loop(0, counts_ref[h, c], add_slot, 0)
    hi, lo = hilo(jnp.concatenate([source[0, 0:SPAN, :], source[1, 0:SPAN, :]], 1))
    fixed[0].wait()
    half = dot(rows_ref[...], jnp.concatenate([hi, lo, hi], 0))
    hi, lo = hilo(half)
    fixed[1].wait()
    spec = dot(jnp.concatenate([hi, lo, hi], 1), cols_ref[...])
    spec_r = spec[:PAD, :PAD] + spec[PAD:, PAD:]
    spec_i = spec[PAD:, :PAD] - spec[:PAD, PAD:]
    fixed[2].wait()
    fixed[3].wait()
    back = []
    for comp in range(2):
        kr = kern[comp, 0]
        ki = kern[comp, 1]
        prod = jnp.concatenate([kr * spec_r - ki * spec_i, kr * spec_i + ki * spec_r], 0)
        hi, lo = hilo(prod)
        t = dot(jnp.concatenate([hi, lo, hi], 1), bcols_ref[...])
        re = t[:PAD, :GRID] - t[PAD:, GRID:]
        im = t[:PAD, GRID:] + t[PAD:, :GRID]
        back.append(jnp.concatenate([re, im], 0))
    hi, lo = hilo(jnp.concatenate(back, 1))
    fixed[4].wait()
    field = dot(brows_ref[...], jnp.concatenate([hi, lo, hi], 0))
    field = jnp.concatenate([field[:, :GRID], field[:, GRID:]], 0)
    hi, lo = hilo(field)
    maps = jnp.concatenate([hi, lo, hi], 1)
    n = pa_ref.shape[-1]
    chunk = 512
    for ref, out_ref, place in (
        (pa_ref, near_ref, 0), (pc_ref, near_ref, 1), (py_ref, far_ref, 0), (pyc_ref, far_ref, 1)
    ):
        for start in range(0, n, chunk):
            both = ref[0, h, :, start : start + chunk]
            x = jnp.where(c == 0, both[0:1], both[1:2])
            both = ref[1, h, :, start : start + chunk]
            y = jnp.where(c == 0, both[0:1], both[1:2])
            hi, lo = hilo(hat(y, chunk))
            t = dot(maps, jnp.concatenate([hi, hi, lo], 0))
            wx = hat(x, chunk)
            kx = jnp.sum(t[:GRID] * wx, axis=0, keepdims=True)
            ky = jnp.sum(t[GRID:] * wx, axis=0, keepdims=True)
            out_ref[place, 0:1, start : start + chunk] = kx
            out_ref[place, 1:2, start : start + chunk] = ky


def field_and_kick(where, partners, offsets, counts, grids, kernel_hat, tables, places):
    n = places[0].shape[-1]
    sm = pl.BlockSpec(memory_space=pltpu.SMEM)
    vm = pl.BlockSpec(memory_space=pltpu.VMEM)
    anyspace = pl.BlockSpec(memory_space=pl.ANY)
    hbm = pl.BlockSpec(memory_space=pltpu.HBM)
    return pl.pallas_call(
        field_body,
        out_shape=[jax.ShapeDtypeStruct((2, 2, n), F32)] * 2,
        in_specs=[sm] * 4 + [anyspace] * 5 + [hbm] * 5 + [vm] * 4,
        out_specs=[vm, vm],
        scratch_shapes=[
            pltpu.VMEM((5, 2, GRID, GRID), F32),
            pltpu.VMEM((2, SPAN + 8, GRID), F32),
            pltpu.VMEM(tables[0].shape, BF),
            pltpu.VMEM(tables[1].shape, BF),
            pltpu.VMEM((2, 2, PAD, PAD), F32),
            pltpu.VMEM(tables[2].shape, BF),
            pltpu.VMEM(tables[3].shape, BF),
            pltpu.SemaphoreType.DMA((5,)),
            pltpu.SemaphoreType.DMA((5,)),
        ],
        compiler_params=pltpu.CompilerParams(vmem_limit_bytes=24 * 1024 * 1024),
        name="field_and_kick",
    )(where, partners, offsets, counts, *grids, kernel_hat, *tables, *places)


def finish_body(where_ref, near_ref, far_ref, nearc_ref, farc_ref, momenta_ref, out_ref):
    h = where_ref[1]
    c = where_ref[2]
    for coord in range(2):
        near = near_ref[0, coord : coord + 1, :]
        nearc = nearc_ref[1, coord : coord + 1, :]
        far = far_ref[0, coord : coord + 1, :]
        farc = farc_ref[1, coord : coord + 1, :]
        for beam in range(2):
            mine = jnp.where(h == beam, near, far)
            other = jnp.where(h == beam, nearc, farc)
            both = jnp.concatenate(
                [jnp.where(c == 0, mine, other), jnp.where(c == 0, other, mine)], 0
            )
            out_ref[coord, beam] = momenta_ref[coord, beam] + both


def finish(where, near, far, nearc, farc, momenta):
    vm = pl.BlockSpec(memory_space=pltpu.VMEM)
    return pl.pallas_call(
        finish_body,
        out_shape=jax.ShapeDtypeStruct(momenta.shape, F32),
        in_specs=[pl.BlockSpec(memory_space=pltpu.SMEM)] + [vm] * 5,
        out_specs=vm,
        compiler_params=pltpu.CompilerParams(vmem_limit_bytes=4 * 1024 * 1024),
        name="finish",
    )(where, near, far, nearc, farc, momenta)


def per_device(positions, momenta, kernel_hat, partners, offsets, counts):
    blocks = lax.axis_size("bunch")
    doms = lax.axis_size("dom")
    b = lax.axis_index("bunch")
    d = lax.axis_index("dom")
    where = jnp.stack([b, d // 2, d % 2, jnp.int32(blocks)]).astype(jnp.int32)

    def across_cores(x):
        return lax.ppermute(x, "dom", [(i, i ^ 1) for i in range(doms)])

    def across_chips(x):
        return lax.ppermute(x, "dom", [(i, i ^ 2) for i in range(doms)])

    def along_blocks(x, by):
        pairs = []
        for i in range(blocks):
            for j in range(doms):
                to = (i + (by if j % 2 == 0 else -by)) % blocks
                pairs.append((i * doms + j, to * doms + j))
        return lax.ppermute(x, ("bunch", "dom"), pairs)

    pos_y = across_chips(positions)
    pos_c = across_cores(positions)
    first = deposit(where, positions, pos_c)
    pos_yc = across_cores(pos_y)
    own = deposit(where, pos_y, pos_yc, first)
    r1 = along_blocks(own, 1)
    r2 = along_blocks(own, 2)
    s1 = across_cores(r1)
    s2 = across_cores(r2)
    tables = [jnp.asarray(t) for t in dft_tables()]
    near, far = field_and_kick(
        where, partners, offsets, counts, (own, r1, r2, s1, s2), kernel_hat, tables,
        (positions, pos_c, pos_y, pos_yc),
    )
    far = across_chips(far)
    nearc = across_cores(near)
    farc = across_cores(far)
    return finish(where, near, far, nearc, farc, momenta)


def solution(mesh):
    in_specs = (
        P(None, None, "bunch", "dom"),
        P(None, None, "bunch", "dom"),
        P(),
        P(None, "bunch", None),
        P(None, None, "bunch", None),
        P(None, "bunch"),
    )
    out_specs = P(None, None, "bunch", "dom")
    return jax.shard_map(
        per_device, mesh=mesh, in_specs=in_specs, out_specs=out_specs, check_vma=False
    )
```

```python
import functools

import jax
import jax.numpy as jnp
import numpy as np
from jax import lax
from jax.experimental import pallas as pl
from jax.experimental.pallas import tpu as pltpu
from jax.sharding import PartitionSpec as P

GRID = 128
PAD = 256
OFFSET = 32
SPAN = GRID + 2 * OFFSET
HALF = 136
HOPS = 2
BF = jnp.bfloat16
F32 = jnp.float32
VM = pl.BlockSpec(memory_space=pltpu.VMEM)
SM = pl.BlockSpec(memory_space=pltpu.SMEM)
HBM = pl.BlockSpec(memory_space=pltpu.HBM)


def in_hbm(x):
    return pltpu.with_memory_space_constraint(x, pltpu.HBM)


def split_const(m):
    hi = m.astype(BF)
    lo = (m - hi.astype(np.float64)).astype(BF)
    return np.asarray(hi), np.asarray(lo)


def dft_tables():
    k = np.arange(PAD)
    w = 2.0 * np.pi / PAD
    half = np.arange(HALF)
    used = (half <= GRID)[:, None]
    r = np.arange(SPAN) - OFFSET
    ang = w * ((half[:, None] * r[None, :]) % PAD)
    hi, lo = split_const(np.concatenate([np.cos(ang) * used, -np.sin(ang) * used], 0))
    rows = np.concatenate([hi, hi, lo], 1)
    r = np.arange(PAD) - OFFSET
    ang = w * ((r[:, None] * k[None, :]) % PAD)
    hi, lo = split_const(np.concatenate([np.cos(ang), np.sin(ang)], 1))
    cols = np.concatenate([hi, hi, lo], 0)
    j = np.arange(GRID)
    ang = w * ((k[:, None] * j[None, :]) % PAD)
    hi, lo = split_const(np.concatenate([np.cos(ang), np.sin(ang)], 1))
    back_cols = np.concatenate([hi, hi, lo], 0)
    ang = w * ((j[:, None] * np.arange(GRID)[None, :]) % PAD)
    re = 2.0 * np.cos(ang)
    re[:, 0] = 1.0
    im = -2.0 * np.sin(ang)
    im[:, 0] = np.cos(np.pi * j)
    hi, lo = split_const(np.concatenate([re, im], 1) / (PAD * PAD))
    back_rows = np.concatenate([hi, hi, lo], 1)
    return rows, cols, back_cols, back_rows


def hilo(v):
    hi = v.astype(BF)
    lo = (v - hi.astype(F32)).astype(BF)
    return hi, lo


def dot(a, b):
    return jnp.dot(a, b, preferred_element_type=F32)


def hat(coord, lanes):
    cells = lax.broadcasted_iota(jnp.int32, (GRID, lanes), 0).astype(F32)
    return jnp.maximum(0.0, 1.0 - jnp.abs(coord - cells))


def chip_half():
    return lax.div(lax.axis_index("dom"), 2)


def core():
    return lax.rem(lax.axis_index("dom"), 2)


def params(mib):
    return pltpu.CompilerParams(vmem_limit_bytes=mib * 1024 * 1024)


def deposit_body(sources, *refs):
    *given, out_ref, tx, ty = refs
    prev_ref = given[sources] if len(given) > sources else None
    e = 1 - chip_half()
    n = given[0].shape[-1]
    for m in range(2):
        for i, ref in enumerate(given[:sources]):
            for coord, table in ((0, tx), (1, ty)):
                hi, lo = hilo(hat(ref[coord, e, pl.ds(m, 1), :], n))
                table[m, 0:GRID, i * n : (i + 1) * n] = hi
                table[m, GRID:, i * n : (i + 1) * n] = lo
        acc = lax.dot_general(
            tx[m], ty[m], (((1,), (1,)), ((), ())), preferred_element_type=F32
        )
        total = (acc[:GRID, :GRID] + acc[GRID:, GRID:]) + (acc[:GRID, GRID:] + acc[GRID:, :GRID])
        if prev_ref is not None:
            total = total + prev_ref[m]
        out_ref[m] = total


def deposit(sources, prev=None):
    n = sources[0].shape[-1]
    args = [*sources] + ([] if prev is None else [prev])
    return pl.pallas_call(
        functools.partial(deposit_body, len(sources)),
        out_shape=jax.ShapeDtypeStruct((2, GRID, GRID), F32),
        in_specs=[VM] * len(args),
        out_specs=VM,
        scratch_shapes=[pltpu.VMEM((2, 2 * GRID, len(sources) * n), BF)] * 2,
        compiler_params=params(16),
        name="deposit",
    )(*args)


def prepare_body(
    pc_ref, py_ref, pyc_ref, pa_hbm, kernel_hbm, half_ref, wx_ref, wy_ref, pa_ref, kernel_ref, sems
):
    own_copy = pltpu.make_async_copy(pa_hbm, pa_ref, sems.at[0])
    kernel_copy = pltpu.make_async_copy(kernel_hbm, kernel_ref, sems.at[1])
    own_copy.start()
    kernel_copy.start()
    h = chip_half()
    c = core()
    n = pa_ref.shape[-1]
    chunk = 512
    for i, ref in ((1, pc_ref), (2, py_ref), (3, pyc_ref), (0, pa_ref)):
        if i == 0:
            own_copy.wait()
        for start in range(0, n, chunk):
            at = slice(i * n + start, i * n + start + chunk)
            both = ref[0, h, :, start : start + chunk]
            wx_ref[:, at] = hat(jnp.where(c == 0, both[0:1], both[1:2]), chunk)
            both = ref[1, h, :, start : start + chunk]
            hi, lo = hilo(hat(jnp.where(c == 0, both[0:1], both[1:2]), chunk))
            wy_ref[0:GRID, at] = hi
            wy_ref[GRID : 2 * GRID, at] = hi
            wy_ref[2 * GRID :, at] = lo
    row = lax.broadcasted_iota(jnp.int32, (PAD, PAD), 0)
    col = lax.broadcasted_iota(jnp.int32, (PAD, PAD), 1)
    flip = jnp.where(((row + col) & (PAD - 1)) == 0, 1.0, 0.0).astype(BF)
    kernel_copy.wait()
    for comp in range(2):
        for part in range(2):
            whole = kernel_ref[comp, part]
            hi, lo = hilo(whole)
            both = jnp.concatenate([dot(flip[:HALF], hi), dot(flip[:HALF], lo)], 0)
            both = dot(both.astype(BF), flip)
            turned = both[:HALF] + both[HALF:]
            if part == 0:
                half_ref[comp, part] = 0.5 * (whole[:HALF] + turned)
            else:
                half_ref[comp, part] = 0.5 * (whole[:HALF] - turned)


def prepare(places, kernel_hat):
    n = 4 * places[0].shape[-1]
    return pl.pallas_call(
        prepare_body,
        out_shape=[
            jax.ShapeDtypeStruct((2, 2, HALF, PAD), F32),
            jax.ShapeDtypeStruct((GRID, n), F32),
            jax.ShapeDtypeStruct((3 * GRID, n), BF),
        ],
        in_specs=[VM] * 3 + [HBM] * 2,
        out_specs=[VM] * 3,
        scratch_shapes=[
            pltpu.VMEM(places[0].shape, F32),
            pltpu.VMEM(kernel_hat.shape, F32),
            pltpu.SemaphoreType.DMA((2,)),
        ],
        compiler_params=params(16),
        name="prepare",
    )(*places[1:], in_hbm(places[0]), in_hbm(kernel_hat))


def field_body(
    partners_hbm, offsets_hbm, counts_hbm,
    own_ref, r1_ref, r2_ref, s1_ref, s2_ref,
    rows_hbm, cols_hbm, bcols_hbm, brows_hbm,
    half_ref, wx_ref, wy_ref,
    out_ref,
    partners_ref, offsets_ref, counts_ref,
    grids, source, rows_ref, cols_ref, bcols_ref, brows_ref, sems,
):
    b = lax.axis_index("bunch")
    ndev = lax.axis_size("bunch")
    h = chip_half()
    c = core()
    fixed = [
        pltpu.make_async_copy(src, dst, sems.at[i])
        for i, (src, dst) in enumerate((
            (partners_hbm, partners_ref), (offsets_hbm, offsets_ref), (counts_hbm, counts_ref),
            (rows_hbm, rows_ref), (cols_hbm, cols_ref),
            (bcols_hbm, bcols_ref), (brows_hbm, brows_ref),
        ))
    ]
    for copy in fixed:
        copy.start()
    places = (2, 1 + 2 * c, 4 * c, 3 - 2 * c, 4 - 4 * c)
    for ref, place in zip((own_ref, r1_ref, r2_ref, s1_ref, s2_ref), places):
        grids[place] = ref[...]
    source[...] = jnp.zeros_like(source)
    lane = lax.broadcasted_iota(jnp.int32, (GRID, GRID), 1)
    for copy in fixed[:3]:
        copy.wait()
    live = counts_ref[h, c]
    for s in range(partners_ref.shape[-1]):
        p = partners_ref[h, c, s]
        rel = lax.rem(lax.div(p, 2) - b + HOPS + 2 * ndev, ndev)
        r0 = offsets_ref[0, h, c, s] + OFFSET
        c0 = offsets_ref[1, h, c, s] + OFFSET
        gain = jnp.where(s < live, 1.0, 0.0)
        turned = pltpu.roll(grids[rel, lax.rem(p, 2)], c0, 1) * gain
        low = jnp.where(lane >= c0, turned, 0.0)
        source[0, pl.ds(r0, GRID), :] += low
        source[1, pl.ds(r0, GRID), :] += turned - low
    hi, lo = hilo(jnp.concatenate([source[0, 0:SPAN, :], source[1, 0:SPAN, :]], 1))
    fixed[3].wait()
    half = dot(rows_ref[...], jnp.concatenate([hi, lo, hi], 0))
    hi, lo = hilo(half)
    fixed[4].wait()
    spec = dot(jnp.concatenate([hi, lo, hi], 1), cols_ref[...])
    spec_r = spec[:HALF, :PAD] + spec[HALF:, PAD:]
    spec_i = spec[HALF:, :PAD] - spec[:HALF, PAD:]
    fixed[5].wait()
    back = []
    for comp in range(2):
        kr = half_ref[comp, 0]
        ki = half_ref[comp, 1]
        prod = jnp.concatenate([kr * spec_r - ki * spec_i, kr * spec_i + ki * spec_r], 0)
        hi, lo = hilo(prod)
        t = dot(jnp.concatenate([hi, lo, hi], 1), bcols_ref[...])
        re = t[:HALF, :GRID] - t[HALF:, GRID:]
        im = t[:GRID, GRID:] + t[HALF : HALF + GRID, :GRID]
        first = lax.broadcasted_iota(jnp.int32, (GRID, GRID), 0) == 0
        im = jnp.where(first, re[GRID : GRID + 1], im)
        back.append(jnp.concatenate([re[:GRID], im], 0))
    hi, lo = hilo(jnp.concatenate(back, 1))
    fixed[6].wait()
    field = dot(brows_ref[...], jnp.concatenate([hi, lo, hi], 0))
    field = jnp.concatenate([field[:, :GRID], field[:, GRID:]], 0)
    hi, lo = hilo(field)
    maps = jnp.concatenate([hi, lo, hi], 1)
    n = out_ref.shape[-1]
    chunk = 512
    for start in range(0, 4 * n, chunk):
        t = dot(maps, wy_ref[:, start : start + chunk])
        wx = wx_ref[:, start : start + chunk]
        at = slice(start % n, start % n + chunk)
        out_ref[start // n, 0:1, at] = jnp.sum(t[:GRID] * wx, axis=0, keepdims=True)
        out_ref[start // n, 1:2, at] = jnp.sum(t[GRID:] * wx, axis=0, keepdims=True)


def field_and_kick(partners, offsets, counts, grids, prepared):
    n = prepared[1].shape[-1] // 4
    tables = [jnp.asarray(t) for t in dft_tables()]
    return pl.pallas_call(
        field_body,
        out_shape=jax.ShapeDtypeStruct((4, 2, n), F32),
        in_specs=[HBM] * 3 + [VM] * 5 + [HBM] * 4 + [VM] * 3,
        out_specs=VM,
        scratch_shapes=[
            *[pltpu.SMEM(t.shape, jnp.int32) for t in (partners, offsets, counts)],
            pltpu.VMEM((2 * HOPS + 1, 2, GRID, GRID), F32),
            pltpu.VMEM((2, SPAN + 8, GRID), F32),
            *[pltpu.VMEM(t.shape, BF) for t in tables],
            pltpu.SemaphoreType.DMA((7,)),
        ],
        compiler_params=params(24),
        name="field_and_kick",
    )(
        in_hbm(partners), in_hbm(offsets), in_hbm(counts), *grids,
        *[in_hbm(t) for t in tables], *prepared,
    )


def finish_body(mine_ref, core_ref, chip_ref, momenta_ref, out_ref):
    h = chip_half()
    c = core()
    for coord in range(2):
        at = slice(coord, coord + 1)
        near = mine_ref[0, at, :]
        nearc = core_ref[1, at, :]
        far = chip_ref[0, at, :]
        farc = chip_ref[1, at, :]
        for beam in range(2):
            same = jnp.where(h == beam, near, far)
            other = jnp.where(h == beam, nearc, farc)
            both = jnp.concatenate(
                [jnp.where(c == 0, same, other), jnp.where(c == 0, other, same)], 0
            )
            out_ref[coord, beam] = momenta_ref[coord, beam] + both


def finish(mine, from_core, from_chip, momenta):
    return pl.pallas_call(
        finish_body,
        out_shape=jax.ShapeDtypeStruct(momenta.shape, F32),
        in_specs=[VM] * 4,
        out_specs=VM,
        compiler_params=params(4),
        name="finish",
    )(mine, from_core, from_chip, momenta)


def per_device(positions, momenta, kernel_hat, partners, offsets, counts):
    blocks = lax.axis_size("bunch")
    doms = lax.axis_size("dom")

    def across_cores(x):
        return lax.ppermute(x, "dom", [(i, i ^ 1) for i in range(doms)])

    def across_chips(x):
        return lax.ppermute(x, "dom", [(i, i ^ 2) for i in range(doms)])

    def along_blocks(x, by):
        pairs = []
        for i in range(blocks):
            for j in range(doms):
                to = (i + (by if j % 2 == 0 else -by)) % blocks
                pairs.append((i * doms + j, to * doms + j))
        return lax.ppermute(x, ("bunch", "dom"), pairs)

    pos_y = across_chips(positions)
    pos_c = across_cores(positions)
    first = deposit([positions, pos_c])
    pos_y, first = lax.optimization_barrier((pos_y, first))
    pos_yc = across_cores(pos_y)
    second = deposit([pos_y], first)
    own = deposit([pos_yc], second)
    own, pos_yc = lax.optimization_barrier((own, pos_yc))
    r1 = along_blocks(own, 1)
    r2 = along_blocks(own, 2)
    prepared = prepare((positions, pos_c, pos_y, pos_yc), kernel_hat)
    r1, prepared = lax.optimization_barrier((r1, prepared))
    s1 = across_cores(r1)
    s2 = across_cores(r2)
    mine = field_and_kick(partners, offsets, counts, (own, r1, r2, s1, s2), prepared)
    from_core = across_cores(mine)
    from_chip = across_chips(jnp.stack([mine[2], from_core[3]]))
    return finish(mine, from_core, from_chip, momenta)


def solution(mesh):
    in_specs = (
        P(None, None, "bunch", "dom"),
        P(None, None, "bunch", "dom"),
        P(),
        P(None, "bunch", None),
        P(None, None, "bunch", None),
        P(None, "bunch"),
    )
    out_specs = P(None, None, "bunch", "dom")
    return jax.shard_map(
        per_device, mesh=mesh, in_specs=in_specs, out_specs=out_specs, check_vma=False
    )
```

```python
import functools

import jax
import jax.numpy as jnp
import numpy as np
from jax import lax
from jax.experimental import pallas as pl
from jax.experimental.pallas import tpu as pltpu
from jax.sharding import PartitionSpec as P

GRID = 128
PAD = 256
OFFSET = 32
SPAN = GRID + 2 * OFFSET
HALF = 136
HOPS = 2
CHUNK = 512
BF = jnp.bfloat16
F32 = jnp.float32
VM = pl.BlockSpec(memory_space=pltpu.VMEM)
SM = pl.BlockSpec(memory_space=pltpu.SMEM)
HBM = pl.BlockSpec(memory_space=pltpu.HBM)


def in_hbm(x):
    return pltpu.with_memory_space_constraint(x, pltpu.HBM)


def split_const(m):
    hi = m.astype(BF)
    lo = (m - hi.astype(np.float64)).astype(BF)
    return np.asarray(hi), np.asarray(lo)


def dft_tables():
    k = np.arange(PAD)
    w = 2.0 * np.pi / PAD
    half = np.arange(HALF)
    used = (half <= GRID)[:, None]
    r = np.arange(SPAN) - OFFSET
    ang = w * ((half[:, None] * r[None, :]) % PAD)
    hi, lo = split_const(np.concatenate([np.cos(ang) * used, -np.sin(ang) * used], 0))
    rows = np.concatenate([hi, hi, lo], 1)
    r = np.arange(PAD) - OFFSET
    ang = w * ((r[:, None] * k[None, :]) % PAD)
    hi, lo = split_const(np.concatenate([np.cos(ang), np.sin(ang)], 1))
    cols = np.concatenate([hi, hi, lo], 0)
    j = np.arange(GRID)
    ang = w * ((k[:, None] * j[None, :]) % PAD)
    hi, lo = split_const(np.concatenate([np.cos(ang), np.sin(ang)], 1))
    back_cols = np.concatenate([hi, hi, lo], 0)
    ang = w * ((j[:, None] * np.arange(GRID)[None, :]) % PAD)
    re = 2.0 * np.cos(ang)
    re[:, 0] = 1.0
    im = -2.0 * np.sin(ang)
    im[:, 0] = np.cos(np.pi * j)
    hi, lo = split_const(np.concatenate([re, im], 1) / (PAD * PAD))
    back_rows = np.concatenate([hi, hi, lo], 1)
    return rows, cols, back_cols, back_rows


def hilo(v):
    hi = v.astype(BF)
    lo = (v - hi.astype(F32)).astype(BF)
    return hi, lo


def dot(a, b):
    return jnp.dot(a, b, preferred_element_type=F32)


def hat(coord, lanes):
    cells = lax.broadcasted_iota(jnp.int32, (GRID, lanes), 0).astype(F32)
    return jnp.maximum(0.0, 1.0 - jnp.abs(coord - cells))


def chip_half():
    return lax.div(lax.axis_index("dom"), 2)


def core():
    return lax.rem(lax.axis_index("dom"), 2)


def params(mib):
    return pltpu.CompilerParams(vmem_limit_bytes=mib * 1024 * 1024)


def deposit_body(sources, *refs):
    *given, out_ref, tx, ty = refs
    prev_ref = given[sources] if len(given) > sources else None
    e = 1 - chip_half()
    n = given[0].shape[-1]
    for m in range(2):
        for i, ref in enumerate(given[:sources]):
            for coord, table in ((0, tx), (1, ty)):
                hi, lo = hilo(hat(ref[coord, e, pl.ds(m, 1), :], n))
                table[m, 0:GRID, i * n : (i + 1) * n] = hi
                table[m, GRID:, i * n : (i + 1) * n] = lo
        acc = lax.dot_general(
            tx[m], ty[m], (((1,), (1,)), ((), ())), preferred_element_type=F32
        )
        total = (acc[:GRID, :GRID] + acc[GRID:, GRID:]) + (acc[:GRID, GRID:] + acc[GRID:, :GRID])
        if prev_ref is not None:
            total = total + prev_ref[m]
        out_ref[m] = total


def deposit(sources, prev=None):
    n = sources[0].shape[-1]
    args = [*sources] + ([] if prev is None else [prev])
    return pl.pallas_call(
        functools.partial(deposit_body, len(sources)),
        out_shape=jax.ShapeDtypeStruct((2, GRID, GRID), F32),
        in_specs=[VM] * len(args),
        out_specs=VM,
        scratch_shapes=[pltpu.VMEM((2, 2 * GRID, len(sources) * n), BF)] * 2,
        compiler_params=params(16),
        name="deposit",
    )(*args)


def prepare_body(
    pc_ref, py_ref, pyc_ref, pa_hbm, kernel_hbm, partners_hbm, offsets_hbm, counts_hbm,
    half_ref, wx_ref, wy_ref, slots_ref,
    pa_ref, kernel_ref, partners_ref, offsets_ref, counts_ref, sems,
):
    small = [
        pltpu.make_async_copy(src, dst, sems.at[i + 2])
        for i, (src, dst) in enumerate((
            (partners_hbm, partners_ref), (offsets_hbm, offsets_ref), (counts_hbm, counts_ref)
        ))
    ]
    for copy in small:
        copy.start()
    own_copy = pltpu.make_async_copy(pa_hbm, pa_ref, sems.at[0])
    kernel_copy = pltpu.make_async_copy(kernel_hbm, kernel_ref, sems.at[1])
    own_copy.start()
    kernel_copy.start()
    h = chip_half()
    c = core()
    n = pa_ref.shape[-1]
    chunk = 512
    for i, ref in ((1, pc_ref), (2, py_ref), (3, pyc_ref), (0, pa_ref)):
        if i == 0:
            own_copy.wait()
        for start in range(0, n, chunk):
            at = slice(i * n + start, i * n + start + chunk)
            both = ref[0, h, :, start : start + chunk]
            wx_ref[:, at] = hat(jnp.where(c == 0, both[0:1], both[1:2]), chunk)
            both = ref[1, h, :, start : start + chunk]
            hi, lo = hilo(hat(jnp.where(c == 0, both[0:1], both[1:2]), chunk))
            wy_ref[0:GRID, at] = hi
            wy_ref[GRID : 2 * GRID, at] = hi
            wy_ref[2 * GRID :, at] = lo
    row = lax.broadcasted_iota(jnp.int32, (PAD, PAD), 0)
    col = lax.broadcasted_iota(jnp.int32, (PAD, PAD), 1)
    flip = jnp.where(((row + col) & (PAD - 1)) == 0, 1.0, 0.0).astype(BF)
    kernel_copy.wait()
    for comp in range(2):
        for part in range(2):
            whole = kernel_ref[comp, part]
            hi, lo = hilo(whole)
            both = jnp.concatenate([dot(flip[:HALF], hi), dot(flip[:HALF], lo)], 0)
            both = dot(both.astype(BF), flip)
            turned = both[:HALF] + both[HALF:]
            if part == 0:
                half_ref[comp, part] = 0.5 * (whole[:HALF] + turned)
            else:
                half_ref[comp, part] = 0.5 * (whole[:HALF] - turned)
    for copy in small:
        copy.wait()
    b = lax.axis_index("bunch")
    ndev = lax.axis_size("bunch")
    live = counts_ref[h, c]
    for s in range(partners_ref.shape[-1]):
        p = partners_ref[h, c, s]
        rel = lax.rem(lax.div(p, 2) - b + HOPS + 2 * ndev, ndev)
        r0 = offsets_ref[0, h, c, s] + OFFSET
        c0 = offsets_ref[1, h, c, s] + OFFSET
        used = jnp.where(s < live, 1, 0)
        code = ((used * 16 + rel * 2 + lax.rem(p, 2)) * 128 + r0) * 128 + c0
        slots_ref[s : s + 1, :] = jnp.full((1, 128), code, jnp.int32)


def prepare(places, kernel_hat, partners, offsets, counts):
    n = 4 * places[0].shape[-1]
    small = (partners, offsets, counts)
    return pl.pallas_call(
        prepare_body,
        out_shape=[
            jax.ShapeDtypeStruct((2, 2, HALF, PAD), F32),
            jax.ShapeDtypeStruct((GRID, n), F32),
            jax.ShapeDtypeStruct((3 * GRID, n), BF),
            jax.ShapeDtypeStruct((partners.shape[-1], 128), jnp.int32),
        ],
        in_specs=[VM] * 3 + [HBM] * 5,
        out_specs=[VM] * 4,
        scratch_shapes=[
            pltpu.VMEM(places[0].shape, F32),
            pltpu.VMEM(kernel_hat.shape, F32),
            *[pltpu.SMEM(t.shape, jnp.int32) for t in small],
            pltpu.SemaphoreType.DMA((5,)),
        ],
        compiler_params=params(16),
        name="prepare",
    )(*places[1:], *[in_hbm(t) for t in (places[0], kernel_hat, *small)])


def kick_of(maps, wx, wy):
    t = dot(maps, wy)
    kx = jnp.sum(t[:GRID] * wx, axis=0, keepdims=True)
    ky = jnp.sum(t[GRID:] * wx, axis=0, keepdims=True)
    return kx, ky


def field_body(
    own_ref, r1_ref, r2_ref, s1_ref, s2_ref,
    rows_hbm, cols_hbm, bcols_hbm, brows_hbm,
    half_ref, wx_ref, wy_ref, slots_ref,
    maps_ref, out_ref,
    grids, source, rows_ref, cols_ref, bcols_ref, brows_ref, sems,
):
    c = core()
    fixed = [
        pltpu.make_async_copy(src, dst, sems.at[i])
        for i, (src, dst) in enumerate((
            (rows_hbm, rows_ref), (cols_hbm, cols_ref),
            (bcols_hbm, bcols_ref), (brows_hbm, brows_ref),
        ))
    ]
    for copy in fixed:
        copy.start()
    slots = slots_ref[...]
    places = (2, 1 + 2 * c, 4 * c, 3 - 2 * c, 4 - 4 * c)
    for ref, place in zip((own_ref, r1_ref, r2_ref, s1_ref, s2_ref), places):
        grids[2 * place] = ref[0]
        grids[2 * place + 1] = ref[1]
    source[...] = jnp.zeros_like(source)
    lane = lax.broadcasted_iota(jnp.int32, (GRID, GRID), 1)
    for s in range(slots_ref.shape[0]):
        code = slots[s, 0]
        c0 = code & 127
        r0 = lax.shift_right_logical(code, 7) & 127
        which = lax.shift_right_logical(code, 14) & 15
        gain = lax.shift_right_logical(code, 18).astype(F32)
        turned = pltpu.roll(grids[which], c0, 1) * gain
        low = jnp.where(lane >= c0, turned, 0.0)
        source[0, pl.ds(r0, GRID), :] += low
        source[1, pl.ds(r0, GRID), :] += turned - low
    hi, lo = hilo(jnp.concatenate([source[0, 0:SPAN, :], source[1, 0:SPAN, :]], 1))
    fixed[0].wait()
    half = dot(rows_ref[...], jnp.concatenate([hi, lo, hi], 0))
    hi, lo = hilo(half)
    fixed[1].wait()
    spec = dot(jnp.concatenate([hi, lo, hi], 1), cols_ref[...])
    spec_r = spec[:HALF, :PAD] + spec[HALF:, PAD:]
    spec_i = spec[HALF:, :PAD] - spec[:HALF, PAD:]
    fixed[2].wait()
    back = []
    for comp in range(2):
        kr = half_ref[comp, 0]
        ki = half_ref[comp, 1]
        prod = jnp.concatenate([kr * spec_r - ki * spec_i, kr * spec_i + ki * spec_r], 0)
        hi, lo = hilo(prod)
        t = dot(jnp.concatenate([hi, lo, hi], 1), bcols_ref[...])
        re = t[:HALF, :GRID] - t[HALF:, GRID:]
        im = t[:GRID, GRID:] + t[HALF : HALF + GRID, :GRID]
        first = lax.broadcasted_iota(jnp.int32, (GRID, GRID), 0) == 0
        im = jnp.where(first, re[GRID : GRID + 1], im)
        back.append(jnp.concatenate([re[:GRID], im], 0))
    hi, lo = hilo(jnp.concatenate(back, 1))
    fixed[3].wait()
    field = dot(brows_ref[...], jnp.concatenate([hi, lo, hi], 0))
    field = jnp.concatenate([field[:, :GRID], field[:, GRID:]], 0)
    hi, lo = hilo(field)
    maps = jnp.concatenate([hi, lo, hi], 1)
    maps_ref[...] = maps
    n = out_ref.shape[-1]
    for start in range(0, n, CHUNK):
        at = slice(3 * n + start, 3 * n + start + CHUNK)
        kx, ky = kick_of(maps, wx_ref[:, at], wy_ref[:, at])
        out_ref[0:1, start : start + CHUNK] = kx
        out_ref[1:2, start : start + CHUNK] = ky


def field(grids, prepared):
    n = prepared[1].shape[-1] // 4
    tables = [jnp.asarray(t) for t in dft_tables()]
    return pl.pallas_call(
        field_body,
        out_shape=[
            jax.ShapeDtypeStruct((2 * GRID, 3 * GRID), BF),
            jax.ShapeDtypeStruct((2, n), F32),
        ],
        in_specs=[VM] * 5 + [HBM] * 4 + [VM] * 4,
        out_specs=[VM] * 2,
        scratch_shapes=[
            pltpu.VMEM((4 * HOPS + 2, GRID, GRID), F32),
            pltpu.VMEM((2, SPAN + 8, GRID), F32),
            *[pltpu.VMEM(t.shape, BF) for t in tables],
            pltpu.SemaphoreType.DMA((4,)),
        ],
        compiler_params=params(24),
        name="field",
    )(*grids, *[in_hbm(t) for t in tables], *prepared)


def kick_body(maps_ref, wx_ref, wy_ref, near_ref, far_ref):
    maps = maps_ref[...]
    n = far_ref.shape[-1]
    for start in range(0, 3 * n, CHUNK):
        at = slice(start, start + CHUNK)
        kx, ky = kick_of(maps, wx_ref[:, at], wy_ref[:, at])
        to = slice(start % n, start % n + CHUNK)
        if start < 2 * n:
            near_ref[start // n, 0:1, to] = kx
            near_ref[start // n, 1:2, to] = ky
        else:
            far_ref[0:1, to] = kx
            far_ref[1:2, to] = ky


def kick(maps, wx, wy):
    n = wx.shape[-1] // 4
    return pl.pallas_call(
        kick_body,
        out_shape=[jax.ShapeDtypeStruct((2, 2, n), F32), jax.ShapeDtypeStruct((2, n), F32)],
        in_specs=[VM] * 3,
        out_specs=[VM] * 2,
        compiler_params=params(8),
        name="kick",
    )(maps, wx, wy)


def finish_body(mine_ref, core_ref, chip_ref, momenta_ref, out_ref):
    h = chip_half()
    c = core()
    for coord in range(2):
        at = slice(coord, coord + 1)
        near = mine_ref[0, at, :]
        nearc = core_ref[1, at, :]
        far = chip_ref[0, at, :]
        farc = chip_ref[1, at, :]
        for beam in range(2):
            same = jnp.where(h == beam, near, far)
            other = jnp.where(h == beam, nearc, farc)
            both = jnp.concatenate(
                [jnp.where(c == 0, same, other), jnp.where(c == 0, other, same)], 0
            )
            out_ref[coord, beam] = momenta_ref[coord, beam] + both


def finish(mine, from_core, from_chip, momenta):
    return pl.pallas_call(
        finish_body,
        out_shape=jax.ShapeDtypeStruct(momenta.shape, F32),
        in_specs=[VM] * 4,
        out_specs=VM,
        compiler_params=params(4),
        name="finish",
    )(mine, from_core, from_chip, momenta)


def per_device(positions, momenta, kernel_hat, partners, offsets, counts):
    blocks = lax.axis_size("bunch")
    doms = lax.axis_size("dom")

    def across_cores(x):
        return lax.ppermute(x, "dom", [(i, i ^ 1) for i in range(doms)])

    def across_chips(x):
        return lax.ppermute(x, "dom", [(i, i ^ 2) for i in range(doms)])

    def along_blocks(x, by):
        pairs = []
        for i in range(blocks):
            for j in range(doms):
                to = (i + (by if j % 2 == 0 else -by)) % blocks
                pairs.append((i * doms + j, to * doms + j))
        return lax.ppermute(x, ("bunch", "dom"), pairs)

    pos_y = across_chips(positions)
    pos_c = across_cores(positions)
    first = deposit([positions, pos_c])
    pos_y, first = lax.optimization_barrier((pos_y, first))
    pos_yc = across_cores(pos_y)
    second = deposit([pos_y], first)
    own = deposit([pos_yc], second)
    own, pos_yc = lax.optimization_barrier((own, pos_yc))
    r1 = along_blocks(own, 1)
    r2 = along_blocks(own, 2)
    prepared = prepare((positions, pos_c, pos_y, pos_yc), kernel_hat, partners, offsets, counts)
    r1, prepared = lax.optimization_barrier((r1, prepared))
    s1 = across_cores(r1)
    r2, s1 = lax.optimization_barrier((r2, s1))
    s2 = across_cores(r2)
    maps, diagonal = field((own, r1, r2, s1, s2), prepared)
    from_core_far = across_cores(diagonal)
    near, far = kick(maps, prepared[1], prepared[2])
    message, mine = lax.optimization_barrier((jnp.stack([far, from_core_far]), near))
    from_chip = across_chips(message)
    from_core = across_cores(mine)
    return finish(mine, from_core, from_chip, momenta)


def solution(mesh):
    in_specs = (
        P(None, None, "bunch", "dom"),
        P(None, None, "bunch", "dom"),
        P(),
        P(None, "bunch", None),
        P(None, None, "bunch", None),
        P(None, "bunch"),
    )
    out_specs = P(None, None, "bunch", "dom")
    return jax.shard_map(
        per_device, mesh=mesh, in_specs=in_specs, out_specs=out_specs, check_vma=False
    )
```

```python
import functools

import jax
import jax.numpy as jnp
import numpy as np
from jax import lax
from jax.experimental import pallas as pl
from jax.experimental.pallas import tpu as pltpu
from jax.sharding import PartitionSpec as P

GRID = 128
PAD = 256
OFFSET = 32
SPAN = GRID + 2 * OFFSET
HALF = 136
HOPS = 2
CHUNK = 512
TILE = 16
DEP_US = 0.01
PACKED_US = 100.0
BF = jnp.bfloat16
F32 = jnp.float32
VM = pl.BlockSpec(memory_space=pltpu.VMEM)
SM = pl.BlockSpec(memory_space=pltpu.SMEM)
HBM = pl.BlockSpec(memory_space=pltpu.HBM)


def in_hbm(x):
    return pltpu.with_memory_space_constraint(x, pltpu.HBM)


def split_const(m):
    hi = m.astype(BF)
    lo = (m - hi.astype(np.float64)).astype(BF)
    return np.asarray(hi), np.asarray(lo)


def dft_tables():
    k = np.arange(PAD)
    w = 2.0 * np.pi / PAD
    half = np.arange(HALF)
    used = (half <= GRID)[:, None]
    r = np.arange(SPAN) - OFFSET
    ang = w * ((half[:, None] * r[None, :]) % PAD)
    hi, lo = split_const(np.concatenate([np.cos(ang) * used, -np.sin(ang) * used], 0))
    rows = np.concatenate([hi, hi, lo], 1)
    r = np.arange(PAD) - OFFSET
    ang = w * ((r[:, None] * k[None, :]) % PAD)
    hi, lo = split_const(np.concatenate([np.cos(ang), np.sin(ang)], 1))
    cols = np.concatenate([hi, hi, lo], 0)
    j = np.arange(GRID)
    ang = w * ((k[:, None] * j[None, :]) % PAD)
    hi, lo = split_const(np.concatenate([np.cos(ang), np.sin(ang)], 1))
    back_cols = np.concatenate([hi, hi, lo], 0)
    ang = w * ((j[:, None] * np.arange(GRID)[None, :]) % PAD)
    re = 2.0 * np.cos(ang)
    re[:, 0] = 1.0
    im = -2.0 * np.sin(ang)
    im[:, 0] = np.cos(np.pi * j)
    hi, lo = split_const(np.concatenate([re, im], 1) / (PAD * PAD))
    back_rows = np.concatenate([hi, hi, lo], 1)
    return rows, cols, back_cols, back_rows


def hilo(v):
    hi = v.astype(BF)
    lo = (v - hi.astype(F32)).astype(BF)
    return hi, lo


def dot(a, b):
    return jnp.dot(a, b, preferred_element_type=F32)


def hat(coord, lanes):
    cells = lax.broadcasted_iota(jnp.int32, (GRID, lanes), 0).astype(F32)
    return jnp.maximum(0.0, 1.0 - jnp.abs(coord - cells))


def hat_split(coord):
    lanes = coord.shape[-1]
    cell = jnp.floor(coord)
    frac = coord - cell
    coarse = jnp.floor(frac * 256.0) * (1.0 / 256.0)
    fine = frac - coarse

    def rows(v):
        return jnp.broadcast_to(v, (TILE, lanes)).astype(BF)

    here, there = rows(cell), rows(cell + 1.0)
    hi = (rows(1.0 - coarse), rows(coarse))
    lo = (rows(-fine), rows(fine))
    zero = jnp.zeros((TILE, lanes), BF)
    base = lax.broadcasted_iota(jnp.int32, (TILE, lanes), 0).astype(F32)
    for start in range(0, GRID, TILE):
        cells = (base + float(start)).astype(BF)
        at_here = cells == here
        at_there = cells == there
        yield (
            slice(start, start + TILE),
            jnp.where(at_here, hi[0], jnp.where(at_there, hi[1], zero)),
            jnp.where(at_here, lo[0], jnp.where(at_there, lo[1], zero)),
        )


def shifted(rows, by):
    return slice(rows.start + by, rows.stop + by)


def chip_half():
    return lax.div(lax.axis_index("dom"), 2)


def core():
    return lax.rem(lax.axis_index("dom"), 2)


def cost(us):
    return pl.CostEstimate(flops=int(us * 1e9), transcendentals=0, bytes_accessed=0)


def params(mib):
    return pltpu.CompilerParams(vmem_limit_bytes=mib * 1024 * 1024)


def deposit_rows(rows, tx, ty):
    for start, coords in rows:
        for coord, table in zip(coords, (tx, ty)):
            n = coord.shape[-1]
            at = slice(start, start + n)
            for cells, hi, lo in hat_split(coord):
                table[cells, at] = hi
                table[shifted(cells, GRID), at] = lo
    return table_product(tx, ty)


def table_product(tx, ty):
    acc = lax.dot_general(
        tx[...], ty[...], (((1,), (1,)), ((), ())), preferred_element_type=F32
    )
    return (acc[:GRID, :GRID] + acc[GRID:, GRID:]) + (acc[:GRID, GRID:] + acc[GRID:, :GRID])


def deposit_body(sources, keep, *refs):
    given = refs[: len(refs) - (4 if keep else 3)]
    out_ref, *kept, tx, ty = refs[len(given) :]
    prev_ref = given[sources] if len(given) > sources else None
    e = 1 - chip_half()
    n = given[0].shape[-1]
    for m in range(2):
        rows = []
        for i, ref in enumerate(given[:sources]):
            for start in range(0, n, CHUNK):
                at = slice(start, start + CHUNK)
                rows.append(
                    (i * n + start, [ref[coord, e, pl.ds(m, 1), at] for coord in range(2)])
                )
        total = deposit_rows(rows, tx.at[m], ty.at[m])
        if prev_ref is not None:
            total = total + prev_ref[m]
        out_ref[m] = total
    for kept_ref in kept:
        for i, ref in enumerate(given[:sources]):
            for coord in range(2):
                kept_ref[i, coord] = ref[coord, e]


def deposit(sources, prev=None, keep=True):
    n = sources[0].shape[-1]
    args = [*sources] + ([] if prev is None else [prev])
    return pl.pallas_call(
        functools.partial(deposit_body, len(sources), keep),
        out_shape=[
            jax.ShapeDtypeStruct((2, GRID, GRID), F32),
            jax.ShapeDtypeStruct((len(sources), 2, 2, n), F32),
        ][: 1 + keep],
        in_specs=[VM] * len(args),
        out_specs=[VM] * (1 + keep),
        scratch_shapes=[pltpu.VMEM((2, 2 * GRID, len(sources) * n), BF)] * 2,
        compiler_params=params(16),
        cost_estimate=cost(DEP_US),
        name="deposit",
    )(*args)


def pack_body(near_ref, y_ref, yc_ref, out_ref):
    e = 1 - chip_half()
    out_ref[0] = near_ref[0]
    out_ref[1] = near_ref[1]
    out_ref[2] = y_ref[0]
    for coord in range(2):
        out_ref[3, coord] = yc_ref[coord, e]


def pack(near, y, yc):
    return pl.pallas_call(
        pack_body,
        out_shape=jax.ShapeDtypeStruct((4, *near.shape[1:]), F32),
        in_specs=[VM] * 3,
        out_specs=VM,
        compiler_params=params(4),
        name="pack",
    )(near, y, yc)


def deposit_packed_body(pos_ref, out_ref, tx, ty):
    sources, _, members, n = pos_ref.shape
    for m in range(members):
        rows = []
        for i in range(sources):
            for start in range(0, n, CHUNK):
                at = slice(start, start + CHUNK)
                rows.append(
                    (i * n + start, [pos_ref[i, coord, m : m + 1, at] for coord in range(2)])
                )
        out_ref[m] = deposit_rows(rows, tx.at[m], ty.at[m])


def deposit_packed(pos):
    return pl.pallas_call(
        deposit_packed_body,
        out_shape=jax.ShapeDtypeStruct((2, GRID, GRID), F32),
        in_specs=[VM],
        out_specs=VM,
        scratch_shapes=[pltpu.VMEM((2, 2 * GRID, pos.shape[0] * pos.shape[-1]), BF)] * 2,
        compiler_params=params(20),
        cost_estimate=cost(PACKED_US),
        name="deposit_packed",
    )(pos)


def first_body(
    pc_ref, pa_hbm, kernel_hbm, partners_hbm, offsets_hbm, counts_hbm,
    out_ref, kept_ref, pa_ref, half_ref, slots_ref,
    tx, ty, kernel_ref, partners_ref, offsets_ref, counts_ref, sems,
):
    copies = [
        pltpu.make_async_copy(src, dst, sems.at[i])
        for i, (src, dst) in enumerate((
            (pa_hbm, pa_ref), (kernel_hbm, kernel_ref), (partners_hbm, partners_ref),
            (offsets_hbm, offsets_ref), (counts_hbm, counts_ref),
        ))
    ]
    for copy in copies:
        copy.start()
    h = chip_half()
    c = core()
    e = 1 - h
    n = pc_ref.shape[-1]
    for i, ref in ((1, pc_ref), (0, pa_ref)):
        if i == 0:
            copies[0].wait()
        for m in range(2):
            for start in range(0, n, CHUNK):
                at = slice(i * n + start, i * n + start + CHUNK)
                for coord, table in ((0, tx), (1, ty)):
                    row = ref[coord, e, pl.ds(m, 1), start : start + CHUNK]
                    for cells, hi, lo in hat_split(row):
                        table[m, cells, at] = hi
                        table[m, shifted(cells, GRID), at] = lo
        for coord in range(2):
            kept_ref[i, coord] = ref[coord, e]
    for m in range(2):
        out_ref[m] = table_product(tx.at[m], ty.at[m])
    row = lax.broadcasted_iota(jnp.int32, (PAD, PAD), 0)
    col = lax.broadcasted_iota(jnp.int32, (PAD, PAD), 1)
    flip = jnp.where(((row + col) & (PAD - 1)) == 0, 1.0, 0.0).astype(BF)
    copies[1].wait()
    for comp in range(2):
        for part in range(2):
            whole = kernel_ref[comp, part]
            hi, lo = hilo(whole)
            both = jnp.concatenate([dot(flip[:HALF], hi), dot(flip[:HALF], lo)], 0)
            both = dot(both.astype(BF), flip)
            turned = both[:HALF] + both[HALF:]
            if part == 0:
                half_ref[comp, part] = 0.5 * (whole[:HALF] + turned)
            else:
                half_ref[comp, part] = 0.5 * (whole[:HALF] - turned)
    for copy in copies[2:]:
        copy.wait()
    b = lax.axis_index("bunch")
    ndev = lax.axis_size("bunch")
    live = counts_ref[h, c]
    for s in range(partners_ref.shape[-1]):
        p = partners_ref[h, c, s]
        rel = lax.rem(lax.div(p, 2) - b + HOPS + 2 * ndev, ndev)
        r0 = offsets_ref[0, h, c, s] + OFFSET
        c0 = offsets_ref[1, h, c, s] + OFFSET
        used = jnp.where(s < live, 1, 0)
        code = ((used * 16 + rel * 2 + lax.rem(p, 2)) * 128 + r0) * 128 + c0
        slots_ref[s : s + 1, :] = jnp.full((1, 128), code, jnp.int32)


def first_deposit(positions, pos_c, kernel_hat, partners, offsets, counts):
    n = positions.shape[-1]
    small = (partners, offsets, counts)
    return pl.pallas_call(
        first_body,
        out_shape=[
            jax.ShapeDtypeStruct((2, GRID, GRID), F32),
            jax.ShapeDtypeStruct((2, 2, 2, n), F32),
            jax.ShapeDtypeStruct(positions.shape, F32),
            jax.ShapeDtypeStruct((2, 2, HALF, PAD), F32),
            jax.ShapeDtypeStruct((partners.shape[-1], 128), jnp.int32),
        ],
        in_specs=[VM] + [HBM] * 5,
        out_specs=[VM] * 5,
        scratch_shapes=[
            *[pltpu.VMEM((2, 2 * GRID, 2 * n), BF)] * 2,
            pltpu.VMEM(kernel_hat.shape, F32),
            *[pltpu.SMEM(t.shape, jnp.int32) for t in small],
            pltpu.SemaphoreType.DMA((5,)),
        ],
        compiler_params=params(16),
        name="first_deposit",
    )(pos_c, *[in_hbm(t) for t in (positions, kernel_hat, *small)])


def kick_tables(ref, start, lanes, wx_ref, wy_ref, to):
    h = chip_half()
    c = core()
    rows = []
    for coord in range(2):
        both = ref[coord, h, :, start : start + lanes]
        rows.append(jnp.where(c == 0, both[0:1], both[1:2]))
    at = slice(to, to + lanes)
    wx_ref[:, at] = hat(rows[0], lanes)
    for cells, hi, lo in hat_split(rows[1]):
        wy_ref[cells, at] = hi
        wy_ref[shifted(cells, GRID), at] = hi
        wy_ref[shifted(cells, 2 * GRID), at] = lo


def kick_of(maps, wx, wy):
    t = dot(maps, wy)
    kx = jnp.sum(t[:GRID] * wx, axis=0, keepdims=True)
    ky = jnp.sum(t[GRID:] * wx, axis=0, keepdims=True)
    return kx, ky


def field_body(
    own_ref, r1_ref, r2_ref, s1_ref, s2_ref,
    rows_hbm, cols_hbm, bcols_hbm, brows_hbm,
    half_ref, slots_ref, pyc_ref,
    maps_ref, out_ref,
    wx_ref, wy_ref, grids, source, rows_ref, cols_ref, bcols_ref, brows_ref, sems,
):
    c = core()
    fixed = [
        pltpu.make_async_copy(src, dst, sems.at[i])
        for i, (src, dst) in enumerate((
            (rows_hbm, rows_ref), (cols_hbm, cols_ref),
            (bcols_hbm, bcols_ref), (brows_hbm, brows_ref),
        ))
    ]
    for copy in fixed:
        copy.start()
    slots = slots_ref[...]
    n = out_ref.shape[-1]
    for start in range(0, n, CHUNK):
        kick_tables(pyc_ref, start, CHUNK, wx_ref, wy_ref, start)
    places = (2, 1 + 2 * c, 4 * c, 3 - 2 * c, 4 - 4 * c)
    for ref, place in zip((own_ref, r1_ref, r2_ref, s1_ref, s2_ref), places):
        grids[2 * place] = ref[0]
        grids[2 * place + 1] = ref[1]
    source[...] = jnp.zeros_like(source)
    lane = lax.broadcasted_iota(jnp.int32, (GRID, GRID), 1)
    for s in range(slots_ref.shape[0]):
        code = slots[s, 0]
        c0 = code & 127
        r0 = lax.shift_right_logical(code, 7) & 127
        which = lax.shift_right_logical(code, 14) & 15
        gain = lax.shift_right_logical(code, 18).astype(F32)
        turned = pltpu.roll(grids[which], c0, 1) * gain
        low = jnp.where(lane >= c0, turned, 0.0)
        source[0, pl.ds(r0, GRID), :] += low
        source[1, pl.ds(r0, GRID), :] += turned - low
    hi, lo = hilo(jnp.concatenate([source[0, 0:SPAN, :], source[1, 0:SPAN, :]], 1))
    fixed[0].wait()
    half = dot(rows_ref[...], jnp.concatenate([hi, lo, hi], 0))
    hi, lo = hilo(half)
    fixed[1].wait()
    spec = dot(jnp.concatenate([hi, lo, hi], 1), cols_ref[...])
    spec_r = spec[:HALF, :PAD] + spec[HALF:, PAD:]
    spec_i = spec[HALF:, :PAD] - spec[:HALF, PAD:]
    fixed[2].wait()
    back = []
    for comp in range(2):
        kr = half_ref[comp, 0]
        ki = half_ref[comp, 1]
        prod = jnp.concatenate([kr * spec_r - ki * spec_i, kr * spec_i + ki * spec_r], 0)
        hi, lo = hilo(prod)
        t = dot(jnp.concatenate([hi, lo, hi], 1), bcols_ref[...])
        re = t[:HALF, :GRID] - t[HALF:, GRID:]
        im = t[:GRID, GRID:] + t[HALF : HALF + GRID, :GRID]
        first = lax.broadcasted_iota(jnp.int32, (GRID, GRID), 0) == 0
        im = jnp.where(first, re[GRID : GRID + 1], im)
        back.append(jnp.concatenate([re[:GRID], im], 0))
    hi, lo = hilo(jnp.concatenate(back, 1))
    fixed[3].wait()
    field = dot(brows_ref[...], jnp.concatenate([hi, lo, hi], 0))
    field = jnp.concatenate([field[:, :GRID], field[:, GRID:]], 0)
    hi, lo = hilo(field)
    maps = jnp.concatenate([hi, lo, hi], 1)
    maps_ref[...] = maps
    for start in range(0, n, CHUNK):
        at = slice(start, start + CHUNK)
        kx, ky = kick_of(maps, wx_ref[:, at], wy_ref[:, at])
        out_ref[0:1, start : start + CHUNK] = kx
        out_ref[1:2, start : start + CHUNK] = ky


def field(grids, half, slots, pos_yc):
    n = pos_yc.shape[-1]
    tables = [jnp.asarray(t) for t in dft_tables()]
    return pl.pallas_call(
        field_body,
        out_shape=[
            jax.ShapeDtypeStruct((2 * GRID, 3 * GRID), BF),
            jax.ShapeDtypeStruct((2, n), F32),
        ],
        in_specs=[VM] * 5 + [HBM] * 4 + [VM] * 3,
        out_specs=[VM] * 2,
        scratch_shapes=[
            pltpu.VMEM((GRID, n), F32),
            pltpu.VMEM((3 * GRID, n), BF),
            pltpu.VMEM((4 * HOPS + 2, GRID, GRID), F32),
            pltpu.VMEM((2, SPAN + 8, GRID), F32),
            *[pltpu.VMEM(t.shape, BF) for t in tables],
            pltpu.SemaphoreType.DMA((4,)),
        ],
        compiler_params=params(24),
        name="field",
    )(*grids, *[in_hbm(t) for t in tables], half, slots, pos_yc)


def kick_body(maps_ref, pa_ref, pc_ref, py_ref, near_ref, far_ref, wx_ref, wy_ref):
    maps = maps_ref[...]
    n = far_ref.shape[-1]
    for i, ref in enumerate((pa_ref, pc_ref, py_ref)):
        for start in range(0, n, CHUNK):
            at = slice(i * n + start, i * n + start + CHUNK)
            kick_tables(ref, start, CHUNK, wx_ref, wy_ref, i * n + start)
            kx, ky = kick_of(maps, wx_ref[:, at], wy_ref[:, at])
            to = slice(start, start + CHUNK)
            if i < 2:
                near_ref[i, 0:1, to] = kx
                near_ref[i, 1:2, to] = ky
            else:
                far_ref[0:1, to] = kx
                far_ref[1:2, to] = ky


def kick(maps, places):
    n = places[0].shape[-1]
    return pl.pallas_call(
        kick_body,
        out_shape=[jax.ShapeDtypeStruct((2, 2, n), F32), jax.ShapeDtypeStruct((2, n), F32)],
        in_specs=[VM] * 4,
        out_specs=[VM] * 2,
        scratch_shapes=[pltpu.VMEM((GRID, 3 * n), F32), pltpu.VMEM((3 * GRID, 3 * n), BF)],
        compiler_params=params(8),
        name="kick",
    )(maps, *places)


def finish_body(mine_ref, core_ref, chip_ref, momenta_ref, out_ref):
    h = chip_half()
    c = core()
    for coord in range(2):
        at = slice(coord, coord + 1)
        near = mine_ref[0, at, :]
        nearc = core_ref[1, at, :]
        far = chip_ref[0, at, :]
        farc = chip_ref[1, at, :]
        for beam in range(2):
            same = jnp.where(h == beam, near, far)
            other = jnp.where(h == beam, nearc, farc)
            both = jnp.concatenate(
                [jnp.where(c == 0, same, other), jnp.where(c == 0, other, same)], 0
            )
            out_ref[coord, beam] = momenta_ref[coord, beam] + both


def finish(mine, from_core, from_chip, momenta):
    return pl.pallas_call(
        finish_body,
        out_shape=jax.ShapeDtypeStruct(momenta.shape, F32),
        in_specs=[VM] * 4,
        out_specs=VM,
        compiler_params=params(4),
        name="finish",
    )(mine, from_core, from_chip, momenta)


def per_device(positions, momenta, kernel_hat, partners, offsets, counts):
    blocks = lax.axis_size("bunch")
    doms = lax.axis_size("dom")

    def across_cores(x):
        return lax.ppermute(x, "dom", [(i, i ^ 1) for i in range(doms)])

    def across_chips(x):
        return lax.ppermute(x, "dom", [(i, i ^ 2) for i in range(doms)])

    def along_blocks(x, by):
        pairs = []
        for i in range(blocks):
            for j in range(doms):
                to = (i + (by if j % 2 == 0 else -by)) % blocks
                pairs.append((i * doms + j, to * doms + j))
        return lax.ppermute(x, ("bunch", "dom"), pairs)

    pos_y = across_chips(positions)
    pos_c = across_cores(positions)
    first, near, pos_own, half, slots = first_deposit(
        positions, pos_c, kernel_hat, partners, offsets, counts
    )
    pos_y, first = lax.optimization_barrier((pos_y, first))
    pos_yc = across_cores(pos_y)
    second, kept_y = deposit([pos_y], first)
    message = pack(near, kept_y, pos_yc)
    p2 = along_blocks(message, 2)
    (own,) = deposit([pos_yc], second, False)
    r1 = along_blocks(own, 1)
    r2 = deposit_packed(p2)
    r1, r2 = lax.optimization_barrier((r1, r2))
    s2 = across_cores(r2)
    s1 = across_cores(r1)
    maps, diagonal = field((own, r1, r2, s1, s2), half, slots, pos_yc)
    from_core_far = across_cores(diagonal)
    near, far = kick(maps, (pos_own, pos_c, pos_y))
    message, mine = lax.optimization_barrier((jnp.stack([far, from_core_far]), near))
    from_chip = across_chips(message)
    from_core = across_cores(mine)
    return finish(mine, from_core, from_chip, momenta)


def solution(mesh):
    in_specs = (
        P(None, None, "bunch", "dom"),
        P(None, None, "bunch", "dom"),
        P(),
        P(None, "bunch", None),
        P(None, None, "bunch", None),
        P(None, "bunch"),
    )
    out_specs = P(None, None, "bunch", "dom")
    return jax.shard_map(
        per_device, mesh=mesh, in_specs=in_specs, out_specs=out_specs, check_vma=False
    )
```

```python
import functools

import jax
import jax.numpy as jnp
import numpy as np
from jax import lax
from jax.experimental import pallas as pl
from jax.experimental.pallas import tpu as pltpu
from jax.sharding import PartitionSpec as P

GRID = 128
PAD = 256
OFFSET = 32
SPAN = GRID + 2 * OFFSET
HALF = 136
HOPS = 2
CHUNK = 512
TILE = 16
DEP_US = 0.01
PACKED_US = 100.0
BF = jnp.bfloat16
F32 = jnp.float32
VM = pl.BlockSpec(memory_space=pltpu.VMEM)
SM = pl.BlockSpec(memory_space=pltpu.SMEM)
HBM = pl.BlockSpec(memory_space=pltpu.HBM)


def in_hbm(x):
    return pltpu.with_memory_space_constraint(x, pltpu.HBM)


def split_const(m):
    hi = m.astype(BF)
    lo = (m - hi.astype(np.float64)).astype(BF)
    return np.asarray(hi), np.asarray(lo)


def dft_tables():
    k = np.arange(PAD)
    w = 2.0 * np.pi / PAD
    half = np.arange(HALF)
    used = (half <= GRID)[:, None]
    r = np.arange(SPAN) - OFFSET
    ang = w * ((half[:, None] * r[None, :]) % PAD)
    hi, lo = split_const(np.concatenate([np.cos(ang) * used, -np.sin(ang) * used], 0))
    rows = np.concatenate([hi, hi, lo], 1)
    r = np.arange(PAD) - OFFSET
    ang = w * ((r[:, None] * k[None, :]) % PAD)
    hi, lo = split_const(np.concatenate([np.cos(ang), np.sin(ang)], 1))
    cols = np.concatenate([hi, hi, lo], 0)
    j = np.arange(GRID)
    ang = w * ((k[:, None] * j[None, :]) % PAD)
    hi, lo = split_const(np.concatenate([np.cos(ang), np.sin(ang)], 1))
    back_cols = np.concatenate([hi, hi, lo], 0)
    ang = w * ((j[:, None] * np.arange(GRID)[None, :]) % PAD)
    re = 2.0 * np.cos(ang)
    re[:, 0] = 1.0
    im = -2.0 * np.sin(ang)
    im[:, 0] = np.cos(np.pi * j)
    hi, lo = split_const(np.concatenate([re, im], 1) / (PAD * PAD))
    back_rows = np.concatenate([hi, hi, lo], 1)
    return rows, cols, back_cols, back_rows


def hilo(v):
    hi = v.astype(BF)
    lo = (v - hi.astype(F32)).astype(BF)
    return hi, lo


def dot(a, b):
    return jnp.dot(a, b, preferred_element_type=F32)


def hat(coord, lanes):
    cells = lax.broadcasted_iota(jnp.int32, (GRID, lanes), 0).astype(F32)
    return jnp.maximum(0.0, 1.0 - jnp.abs(coord - cells))


def hat_split(coord):
    lanes = coord.shape[-1]
    cell = jnp.floor(coord)
    frac = coord - cell
    coarse = jnp.floor(frac * 256.0) * (1.0 / 256.0)
    fine = frac - coarse

    def rows(v):
        return jnp.broadcast_to(v, (TILE, lanes)).astype(BF)

    here, there = rows(cell), rows(cell + 1.0)
    hi = (rows(1.0 - coarse), rows(coarse))
    lo = (rows(-fine), rows(fine))
    zero = jnp.zeros((TILE, lanes), BF)
    base = lax.broadcasted_iota(jnp.int32, (TILE, lanes), 0).astype(F32)
    for start in range(0, GRID, TILE):
        cells = (base + float(start)).astype(BF)
        at_here = cells == here
        at_there = cells == there
        yield (
            slice(start, start + TILE),
            jnp.where(at_here, hi[0], jnp.where(at_there, hi[1], zero)),
            jnp.where(at_here, lo[0], jnp.where(at_there, lo[1], zero)),
        )


def shifted(rows, by):
    return slice(rows.start + by, rows.stop + by)


def chip_half():
    return lax.div(lax.axis_index("dom"), 2)


def core():
    return lax.rem(lax.axis_index("dom"), 2)


def cost(us):
    return pl.CostEstimate(flops=int(us * 1e9), transcendentals=0, bytes_accessed=0)


def params(mib):
    return pltpu.CompilerParams(vmem_limit_bytes=mib * 1024 * 1024)


def deposit_rows(rows, tx, ty):
    for start, coords in rows:
        for coord, table in zip(coords, (tx, ty)):
            n = coord.shape[-1]
            at = slice(start, start + n)
            for cells, hi, lo in hat_split(coord):
                table[cells, at] = hi
                table[shifted(cells, GRID), at] = lo
    return table_product(tx, ty)


def table_product(tx, ty):
    acc = lax.dot_general(
        tx[...], ty[...], (((1,), (1,)), ((), ())), preferred_element_type=F32
    )
    return (acc[:GRID, :GRID] + acc[GRID:, GRID:]) + (acc[:GRID, GRID:] + acc[GRID:, :GRID])


def deposit_body(sources, keep, *refs):
    given = refs[: len(refs) - (4 if keep else 3)]
    out_ref, *kept, tx, ty = refs[len(given) :]
    prev_ref = given[sources] if len(given) > sources else None
    e = 1 - chip_half()
    n = given[0].shape[-1]
    for m in range(2):
        rows = []
        for i, ref in enumerate(given[:sources]):
            for start in range(0, n, CHUNK):
                at = slice(start, start + CHUNK)
                rows.append(
                    (i * n + start, [ref[coord, e, pl.ds(m, 1), at] for coord in range(2)])
                )
        total = deposit_rows(rows, tx.at[m], ty.at[m])
        if prev_ref is not None:
            total = total + prev_ref[m]
        out_ref[m] = total
    for kept_ref in kept:
        for i, ref in enumerate(given[:sources]):
            for coord in range(2):
                kept_ref[i, coord] = ref[coord, e]


def deposit(sources, prev=None, keep=True):
    n = sources[0].shape[-1]
    args = [*sources] + ([] if prev is None else [prev])
    return pl.pallas_call(
        functools.partial(deposit_body, len(sources), keep),
        out_shape=[
            jax.ShapeDtypeStruct((2, GRID, GRID), F32),
            jax.ShapeDtypeStruct((len(sources), 2, 2, n), F32),
        ][: 1 + keep],
        in_specs=[VM] * len(args),
        out_specs=[VM] * (1 + keep),
        scratch_shapes=[pltpu.VMEM((2, 2 * GRID, len(sources) * n), BF)] * 2,
        compiler_params=params(16),
        cost_estimate=cost(DEP_US),
        name="deposit",
    )(*args)


def pack_body(near_ref, y_ref, yc_ref, out_ref):
    e = 1 - chip_half()
    out_ref[0] = near_ref[0]
    out_ref[1] = near_ref[1]
    out_ref[2] = y_ref[0]
    for coord in range(2):
        out_ref[3, coord] = yc_ref[coord, e]


def pack(near, y, yc):
    return pl.pallas_call(
        pack_body,
        out_shape=jax.ShapeDtypeStruct((4, *near.shape[1:]), F32),
        in_specs=[VM] * 3,
        out_specs=VM,
        compiler_params=params(4),
        name="pack",
    )(near, y, yc)


def deposit_packed_body(pos_ref, out_ref, tx, ty):
    sources, _, members, n = pos_ref.shape
    for m in range(members):
        rows = []
        for i in range(sources):
            for start in range(0, n, CHUNK):
                at = slice(start, start + CHUNK)
                rows.append(
                    (i * n + start, [pos_ref[i, coord, m : m + 1, at] for coord in range(2)])
                )
        out_ref[m] = deposit_rows(rows, tx.at[m], ty.at[m])


def deposit_packed(pos):
    return pl.pallas_call(
        deposit_packed_body,
        out_shape=jax.ShapeDtypeStruct((2, GRID, GRID), F32),
        in_specs=[VM],
        out_specs=VM,
        scratch_shapes=[pltpu.VMEM((2, 2 * GRID, pos.shape[0] * pos.shape[-1]), BF)] * 2,
        compiler_params=params(20),
        cost_estimate=cost(PACKED_US),
        name="deposit_packed",
    )(pos)


def first_body(
    pc_ref, pa_hbm, kernel_hbm, partners_hbm, offsets_hbm, counts_hbm,
    rows_hbm, cols_hbm, bcols_hbm, brows_hbm,
    out_ref, kept_ref, pa_ref, half_ref, slots_ref, rows_ref, cols_ref, bcols_ref, brows_ref,
    tx, ty, kernel_ref, partners_ref, offsets_ref, counts_ref, sems,
):
    copies = [
        pltpu.make_async_copy(src, dst, sems.at[i])
        for i, (src, dst) in enumerate((
            (pa_hbm, pa_ref), (kernel_hbm, kernel_ref), (partners_hbm, partners_ref),
            (offsets_hbm, offsets_ref), (counts_hbm, counts_ref), (rows_hbm, rows_ref),
            (cols_hbm, cols_ref), (bcols_hbm, bcols_ref), (brows_hbm, brows_ref),
        ))
    ]
    for copy in copies:
        copy.start()
    h = chip_half()
    c = core()
    e = 1 - h
    n = pc_ref.shape[-1]
    for i, ref in ((1, pc_ref), (0, pa_ref)):
        if i == 0:
            copies[0].wait()
        for m in range(2):
            for start in range(0, n, CHUNK):
                at = slice(i * n + start, i * n + start + CHUNK)
                for coord, table in ((0, tx), (1, ty)):
                    row = ref[coord, e, pl.ds(m, 1), start : start + CHUNK]
                    for cells, hi, lo in hat_split(row):
                        table[m, cells, at] = hi
                        table[m, shifted(cells, GRID), at] = lo
        for coord in range(2):
            kept_ref[i, coord] = ref[coord, e]
    for m in range(2):
        out_ref[m] = table_product(tx.at[m], ty.at[m])
    row = lax.broadcasted_iota(jnp.int32, (PAD, PAD), 0)
    col = lax.broadcasted_iota(jnp.int32, (PAD, PAD), 1)
    flip = jnp.where(((row + col) & (PAD - 1)) == 0, 1.0, 0.0).astype(BF)
    copies[1].wait()
    for comp in range(2):
        for part in range(2):
            whole = kernel_ref[comp, part]
            hi, lo = hilo(whole)
            both = jnp.concatenate([dot(flip[:HALF], hi), dot(flip[:HALF], lo)], 0)
            both = dot(both.astype(BF), flip)
            turned = both[:HALF] + both[HALF:]
            if part == 0:
                half_ref[comp, part] = 0.5 * (whole[:HALF] + turned)
            else:
                half_ref[comp, part] = 0.5 * (whole[:HALF] - turned)
    for copy in copies[2:]:
        copy.wait()
    b = lax.axis_index("bunch")
    ndev = lax.axis_size("bunch")
    live = counts_ref[h, c]
    for s in range(partners_ref.shape[-1]):
        p = partners_ref[h, c, s]
        rel = lax.rem(lax.div(p, 2) - b + HOPS + 2 * ndev, ndev)
        r0 = offsets_ref[0, h, c, s] + OFFSET
        c0 = offsets_ref[1, h, c, s] + OFFSET
        used = jnp.where(s < live, 1, 0)
        code = ((used * 16 + rel * 2 + lax.rem(p, 2)) * 128 + r0) * 128 + c0
        slots_ref[s : s + 1, :] = jnp.full((1, 128), code, jnp.int32)


def first_deposit(positions, pos_c, kernel_hat, partners, offsets, counts):
    n = positions.shape[-1]
    small = (partners, offsets, counts)
    tables = [jnp.asarray(t) for t in dft_tables()]
    return pl.pallas_call(
        first_body,
        out_shape=[
            jax.ShapeDtypeStruct((2, GRID, GRID), F32),
            jax.ShapeDtypeStruct((2, 2, 2, n), F32),
            jax.ShapeDtypeStruct(positions.shape, F32),
            jax.ShapeDtypeStruct((2, 2, HALF, PAD), F32),
            jax.ShapeDtypeStruct((partners.shape[-1], 128), jnp.int32),
            *[jax.ShapeDtypeStruct(t.shape, BF) for t in tables],
        ],
        in_specs=[VM] + [HBM] * 9,
        out_specs=[VM] * 9,
        scratch_shapes=[
            *[pltpu.VMEM((2, 2 * GRID, 2 * n), BF)] * 2,
            pltpu.VMEM(kernel_hat.shape, F32),
            *[pltpu.SMEM(t.shape, jnp.int32) for t in small],
            pltpu.SemaphoreType.DMA((9,)),
        ],
        compiler_params=params(16),
        name="first_deposit",
    )(pos_c, *[in_hbm(t) for t in (positions, kernel_hat, *small, *tables)])


def kick_tables(ref, start, lanes, wx_ref, wy_ref, to):
    h = chip_half()
    c = core()
    rows = []
    for coord in range(2):
        both = ref[coord, h, :, start : start + lanes]
        rows.append(jnp.where(c == 0, both[0:1], both[1:2]))
    at = slice(to, to + lanes)
    wx_ref[:, at] = hat(rows[0], lanes)
    for cells, hi, lo in hat_split(rows[1]):
        wy_ref[cells, at] = hi
        wy_ref[shifted(cells, GRID), at] = hi
        wy_ref[shifted(cells, 2 * GRID), at] = lo


def kick_of(maps, wx, wy):
    t = dot(maps, wy)
    kx = jnp.sum(t[:GRID] * wx, axis=0, keepdims=True)
    ky = jnp.sum(t[GRID:] * wx, axis=0, keepdims=True)
    return kx, ky


def field_body(
    own_ref, r1_ref, r2_ref, s1_ref, s2_ref,
    half_ref, slots_ref, rows_ref, cols_ref, bcols_ref, brows_ref, pyc_ref,
    maps_ref, out_ref,
    wx_ref, wy_ref, grids, source,
):
    c = core()
    slots = slots_ref[...]
    n = out_ref.shape[-1]
    for start in range(0, n, CHUNK):
        kick_tables(pyc_ref, start, CHUNK, wx_ref, wy_ref, start)
    places = (2, 1 + 2 * c, 4 * c, 3 - 2 * c, 4 - 4 * c)
    for ref, place in zip((own_ref, r1_ref, r2_ref, s1_ref, s2_ref), places):
        grids[2 * place] = ref[0]
        grids[2 * place + 1] = ref[1]
    source[...] = jnp.zeros_like(source)
    lane = lax.broadcasted_iota(jnp.int32, (GRID, GRID), 1)
    for s in range(slots_ref.shape[0]):
        code = slots[s, 0]
        c0 = code & 127
        r0 = lax.shift_right_logical(code, 7) & 127
        which = lax.shift_right_logical(code, 14) & 15
        gain = lax.shift_right_logical(code, 18).astype(F32)
        turned = pltpu.roll(grids[which], c0, 1) * gain
        low = jnp.where(lane >= c0, turned, 0.0)
        source[0, pl.ds(r0, GRID), :] += low
        source[1, pl.ds(r0, GRID), :] += turned - low
    hi, lo = hilo(jnp.concatenate([source[0, 0:SPAN, :], source[1, 0:SPAN, :]], 1))
    half = dot(rows_ref[...], jnp.concatenate([hi, lo, hi], 0))
    hi, lo = hilo(half)
    spec = dot(jnp.concatenate([hi, lo, hi], 1), cols_ref[...])
    spec_r = spec[:HALF, :PAD] + spec[HALF:, PAD:]
    spec_i = spec[HALF:, :PAD] - spec[:HALF, PAD:]
    back = []
    for comp in range(2):
        kr = half_ref[comp, 0]
        ki = half_ref[comp, 1]
        prod = jnp.concatenate([kr * spec_r - ki * spec_i, kr * spec_i + ki * spec_r], 0)
        hi, lo = hilo(prod)
        t = dot(jnp.concatenate([hi, lo, hi], 1), bcols_ref[...])
        re = t[:HALF, :GRID] - t[HALF:, GRID:]
        im = t[:GRID, GRID:] + t[HALF : HALF + GRID, :GRID]
        first = lax.broadcasted_iota(jnp.int32, (GRID, GRID), 0) == 0
        im = jnp.where(first, re[GRID : GRID + 1], im)
        back.append(jnp.concatenate([re[:GRID], im], 0))
    hi, lo = hilo(jnp.concatenate(back, 1))
    field = dot(brows_ref[...], jnp.concatenate([hi, lo, hi], 0))
    field = jnp.concatenate([field[:, :GRID], field[:, GRID:]], 0)
    hi, lo = hilo(field)
    maps = jnp.concatenate([hi, lo, hi], 1)
    maps_ref[...] = maps
    for start in range(0, n, CHUNK):
        at = slice(start, start + CHUNK)
        kx, ky = kick_of(maps, wx_ref[:, at], wy_ref[:, at])
        out_ref[0:1, start : start + CHUNK] = kx
        out_ref[1:2, start : start + CHUNK] = ky


def field(grids, half, slots, tables, pos_yc):
    n = pos_yc.shape[-1]
    return pl.pallas_call(
        field_body,
        out_shape=[
            jax.ShapeDtypeStruct((2 * GRID, 3 * GRID), BF),
            jax.ShapeDtypeStruct((2, n), F32),
        ],
        in_specs=[VM] * 12,
        out_specs=[VM] * 2,
        scratch_shapes=[
            pltpu.VMEM((GRID, n), F32),
            pltpu.VMEM((3 * GRID, n), BF),
            pltpu.VMEM((4 * HOPS + 2, GRID, GRID), F32),
            pltpu.VMEM((2, SPAN + 8, GRID), F32),
        ],
        compiler_params=params(24),
        name="field",
    )(*grids, half, slots, *tables, pos_yc)


def kick_body(maps_ref, pa_ref, pc_ref, py_ref, near_ref, far_ref, wx_ref, wy_ref):
    maps = maps_ref[...]
    n = far_ref.shape[-1]
    for i, ref in enumerate((pa_ref, pc_ref, py_ref)):
        for start in range(0, n, CHUNK):
            at = slice(i * n + start, i * n + start + CHUNK)
            kick_tables(ref, start, CHUNK, wx_ref, wy_ref, i * n + start)
            kx, ky = kick_of(maps, wx_ref[:, at], wy_ref[:, at])
            to = slice(start, start + CHUNK)
            if i < 2:
                near_ref[i, 0:1, to] = kx
                near_ref[i, 1:2, to] = ky
            else:
                far_ref[0:1, to] = kx
                far_ref[1:2, to] = ky


def kick(maps, places):
    n = places[0].shape[-1]
    return pl.pallas_call(
        kick_body,
        out_shape=[jax.ShapeDtypeStruct((2, 2, n), F32), jax.ShapeDtypeStruct((2, n), F32)],
        in_specs=[VM] * 4,
        out_specs=[VM] * 2,
        scratch_shapes=[pltpu.VMEM((GRID, 3 * n), F32), pltpu.VMEM((3 * GRID, 3 * n), BF)],
        compiler_params=params(8),
        name="kick",
    )(maps, *places)


def finish_body(mine_ref, core_ref, chip_ref, momenta_ref, out_ref):
    h = chip_half()
    c = core()
    for coord in range(2):
        at = slice(coord, coord + 1)
        near = mine_ref[0, at, :]
        nearc = core_ref[1, at, :]
        far = chip_ref[0, at, :]
        farc = chip_ref[1, at, :]
        for beam in range(2):
            same = jnp.where(h == beam, near, far)
            other = jnp.where(h == beam, nearc, farc)
            both = jnp.concatenate(
                [jnp.where(c == 0, same, other), jnp.where(c == 0, other, same)], 0
            )
            out_ref[coord, beam] = momenta_ref[coord, beam] + both


def finish(mine, from_core, from_chip, momenta):
    return pl.pallas_call(
        finish_body,
        out_shape=jax.ShapeDtypeStruct(momenta.shape, F32),
        in_specs=[VM] * 4,
        out_specs=VM,
        compiler_params=params(4),
        name="finish",
    )(mine, from_core, from_chip, momenta)


def per_device(positions, momenta, kernel_hat, partners, offsets, counts):
    blocks = lax.axis_size("bunch")
    doms = lax.axis_size("dom")

    def across_cores(x):
        return lax.ppermute(x, "dom", [(i, i ^ 1) for i in range(doms)])

    def across_chips(x):
        return lax.ppermute(x, "dom", [(i, i ^ 2) for i in range(doms)])

    def along_blocks(x, by):
        pairs = []
        for i in range(blocks):
            for j in range(doms):
                to = (i + (by if j % 2 == 0 else -by)) % blocks
                pairs.append((i * doms + j, to * doms + j))
        return lax.ppermute(x, ("bunch", "dom"), pairs)

    pos_y = across_chips(positions)
    pos_c = across_cores(positions)
    first, near, pos_own, half, slots, *tables = first_deposit(
        positions, pos_c, kernel_hat, partners, offsets, counts
    )
    pos_y, first = lax.optimization_barrier((pos_y, first))
    pos_yc = across_cores(pos_y)
    second, kept_y = deposit([pos_y], first)
    message = pack(near, kept_y, pos_yc)
    p2 = along_blocks(message, 2)
    (own,) = deposit([pos_yc], second, False)
    r1 = along_blocks(own, 1)
    r2 = deposit_packed(p2)
    r1, r2 = lax.optimization_barrier((r1, r2))
    s2 = across_cores(r2)
    s1 = across_cores(r1)
    maps, diagonal = field((own, r1, r2, s1, s2), half, slots, tables, pos_yc)
    from_core_far = across_cores(diagonal)
    near, far = kick(maps, (pos_own, pos_c, pos_y))
    message, mine = lax.optimization_barrier((jnp.stack([far, from_core_far]), near))
    from_chip = across_chips(message)
    from_core = across_cores(mine)
    return finish(mine, from_core, from_chip, momenta)


def solution(mesh):
    in_specs = (
        P(None, None, "bunch", "dom"),
        P(None, None, "bunch", "dom"),
        P(),
        P(None, "bunch", None),
        P(None, None, "bunch", None),
        P(None, "bunch"),
    )
    out_specs = P(None, None, "bunch", "dom")
    return jax.shard_map(
        per_device, mesh=mesh, in_specs=in_specs, out_specs=out_specs, check_vma=False
    )
```

```python
import functools

import jax
import jax.numpy as jnp
import numpy as np
from jax import lax
from jax.experimental import pallas as pl
from jax.experimental.pallas import tpu as pltpu
from jax.sharding import PartitionSpec as P

GRID = 128
PAD = 256
OFFSET = 32
SPAN = GRID + 2 * OFFSET
HALF = 136
HOPS = 2
CHUNK = 512
TILE = 16
DEP_US = 0.01
PACKED_US = 100.0
BF = jnp.bfloat16
F32 = jnp.float32
VM = pl.BlockSpec(memory_space=pltpu.VMEM)
SM = pl.BlockSpec(memory_space=pltpu.SMEM)
HBM = pl.BlockSpec(memory_space=pltpu.HBM)


def in_hbm(x):
    return pltpu.with_memory_space_constraint(x, pltpu.HBM)


def split_const(m):
    hi = m.astype(BF)
    lo = (m - hi.astype(np.float64)).astype(BF)
    return np.asarray(hi), np.asarray(lo)


def dft_tables():
    k = np.arange(PAD)
    w = 2.0 * np.pi / PAD
    half = np.arange(HALF)
    used = (half <= GRID)[:, None]
    r = np.arange(SPAN) - OFFSET
    ang = w * ((half[:, None] * r[None, :]) % PAD)
    hi, lo = split_const(np.concatenate([np.cos(ang) * used, -np.sin(ang) * used], 0))
    rows = np.concatenate([hi, hi, lo], 1)
    r = np.arange(PAD) - OFFSET
    ang = w * ((r[:, None] * k[None, :]) % PAD)
    hi, lo = split_const(np.concatenate([np.cos(ang), np.sin(ang)], 1))
    cols = np.concatenate([hi, hi, lo], 0)
    j = np.arange(GRID)
    ang = w * ((k[:, None] * j[None, :]) % PAD)
    hi, lo = split_const(np.concatenate([np.cos(ang), np.sin(ang)], 1))
    back_cols = np.concatenate([hi, hi, lo], 0)
    ang = w * ((j[:, None] * np.arange(GRID)[None, :]) % PAD)
    re = 2.0 * np.cos(ang)
    re[:, 0] = 1.0
    im = -2.0 * np.sin(ang)
    im[:, 0] = np.cos(np.pi * j)
    hi, lo = split_const(np.concatenate([re, im], 1) / (PAD * PAD))
    back_rows = np.concatenate([hi, hi, lo], 1)
    return rows, cols, back_cols, back_rows


def hilo(v):
    hi = v.astype(BF)
    lo = (v - hi.astype(F32)).astype(BF)
    return hi, lo


def dot(a, b):
    return jnp.dot(a, b, preferred_element_type=F32)


def hat(coord, lanes):
    cells = lax.broadcasted_iota(jnp.int32, (GRID, lanes), 0).astype(F32)
    return jnp.maximum(0.0, 1.0 - jnp.abs(coord - cells))


def hat_split(coord):
    lanes = coord.shape[-1]
    cell = jnp.floor(coord)
    frac = coord - cell
    coarse = jnp.floor(frac * 256.0) * (1.0 / 256.0)
    fine = frac - coarse

    def rows(v):
        return jnp.broadcast_to(v, (TILE, lanes)).astype(BF)

    here, there = rows(cell), rows(cell + 1.0)
    hi = (rows(1.0 - coarse), rows(coarse))
    lo = (rows(-fine), rows(fine))
    zero = jnp.zeros((TILE, lanes), BF)
    base = lax.broadcasted_iota(jnp.int32, (TILE, lanes), 0).astype(F32)
    for start in range(0, GRID, TILE):
        cells = (base + float(start)).astype(BF)
        at_here = cells == here
        at_there = cells == there
        yield (
            slice(start, start + TILE),
            jnp.where(at_here, hi[0], jnp.where(at_there, hi[1], zero)),
            jnp.where(at_here, lo[0], jnp.where(at_there, lo[1], zero)),
        )


def shifted(rows, by):
    return slice(rows.start + by, rows.stop + by)


def chip_half():
    return lax.div(lax.axis_index("dom"), 2)


def core():
    return lax.rem(lax.axis_index("dom"), 2)


def cost(us):
    return pl.CostEstimate(flops=int(us * 1e9), transcendentals=0, bytes_accessed=0)


def params(mib):
    return pltpu.CompilerParams(vmem_limit_bytes=mib * 1024 * 1024)


def deposit_rows(rows, tx, ty):
    for start, coords in rows:
        for coord, table in zip(coords, (tx, ty)):
            n = coord.shape[-1]
            at = slice(start, start + n)
            for cells, hi, lo in hat_split(coord):
                table[cells, at] = hi
                table[shifted(cells, GRID), at] = lo
    return table_product(tx, ty)


def table_product(tx, ty):
    acc = lax.dot_general(
        tx[...], ty[...], (((1,), (1,)), ((), ())), preferred_element_type=F32
    )
    return (acc[:GRID, :GRID] + acc[GRID:, GRID:]) + (acc[:GRID, GRID:] + acc[GRID:, :GRID])


def deposit_body(sources, keep, *refs):
    given = refs[: len(refs) - (4 if keep else 3)]
    out_ref, *kept, tx, ty = refs[len(given) :]
    prev_ref = given[sources] if len(given) > sources else None
    e = 1 - chip_half()
    n = given[0].shape[-1]
    for m in range(2):
        rows = []
        for i, ref in enumerate(given[:sources]):
            for start in range(0, n, CHUNK):
                at = slice(start, start + CHUNK)
                rows.append(
                    (i * n + start, [ref[coord, e, pl.ds(m, 1), at] for coord in range(2)])
                )
        total = deposit_rows(rows, tx.at[m], ty.at[m])
        if prev_ref is not None:
            total = total + prev_ref[m]
        out_ref[m] = total
    for kept_ref in kept:
        for i, ref in enumerate(given[:sources]):
            for coord in range(2):
                kept_ref[i, coord] = ref[coord, e]


def deposit(sources, prev=None, keep=True):
    n = sources[0].shape[-1]
    args = [*sources] + ([] if prev is None else [prev])
    return pl.pallas_call(
        functools.partial(deposit_body, len(sources), keep),
        out_shape=[
            jax.ShapeDtypeStruct((2, GRID, GRID), F32),
            jax.ShapeDtypeStruct((len(sources), 2, 2, n), F32),
        ][: 1 + keep],
        in_specs=[VM] * len(args),
        out_specs=[VM] * (1 + keep),
        scratch_shapes=[pltpu.VMEM((2, 2 * GRID, len(sources) * n), BF)] * 2,
        compiler_params=params(16),
        cost_estimate=cost(DEP_US),
        name="deposit",
    )(*args)


def pack_body(near_ref, y_ref, yc_ref, out_ref):
    e = 1 - chip_half()
    out_ref[0] = near_ref[0]
    out_ref[1] = near_ref[1]
    out_ref[2] = y_ref[0]
    for coord in range(2):
        out_ref[3, coord] = yc_ref[coord, e]


def pack(near, y, yc):
    return pl.pallas_call(
        pack_body,
        out_shape=jax.ShapeDtypeStruct((4, *near.shape[1:]), F32),
        in_specs=[VM] * 3,
        out_specs=VM,
        compiler_params=params(4),
        name="pack",
    )(near, y, yc)


def deposit_packed_body(pos_ref, out_ref, tx, ty):
    sources, _, members, n = pos_ref.shape
    for m in range(members):
        rows = []
        for i in range(sources):
            for start in range(0, n, CHUNK):
                at = slice(start, start + CHUNK)
                rows.append(
                    (i * n + start, [pos_ref[i, coord, m : m + 1, at] for coord in range(2)])
                )
        out_ref[m] = deposit_rows(rows, tx.at[m], ty.at[m])


def deposit_packed(pos):
    return pl.pallas_call(
        deposit_packed_body,
        out_shape=jax.ShapeDtypeStruct((2, GRID, GRID), F32),
        in_specs=[VM],
        out_specs=VM,
        scratch_shapes=[pltpu.VMEM((2, 2 * GRID, pos.shape[0] * pos.shape[-1]), BF)] * 2,
        compiler_params=params(20),
        cost_estimate=cost(PACKED_US),
        name="deposit_packed",
    )(pos)


def first_body(
    pc_ref, pa_hbm, kernel_hbm, partners_hbm, offsets_hbm, counts_hbm,
    rows_hbm, cols_hbm, bcols_hbm, brows_hbm,
    out_ref, kept_ref, pa_ref, half_ref, slots_ref, rows_ref, cols_ref, bcols_ref, brows_ref,
    tx, ty, kernel_ref, partners_ref, offsets_ref, counts_ref, sems,
):
    copies = [
        pltpu.make_async_copy(src, dst, sems.at[i])
        for i, (src, dst) in enumerate((
            (pa_hbm, pa_ref), (kernel_hbm, kernel_ref), (partners_hbm, partners_ref),
            (offsets_hbm, offsets_ref), (counts_hbm, counts_ref), (rows_hbm, rows_ref),
            (cols_hbm, cols_ref), (bcols_hbm, bcols_ref), (brows_hbm, brows_ref),
        ))
    ]
    for copy in copies:
        copy.start()
    h = chip_half()
    c = core()
    e = 1 - h
    n = pc_ref.shape[-1]
    for i, ref in ((1, pc_ref), (0, pa_ref)):
        if i == 0:
            copies[0].wait()
        for m in range(2):
            for start in range(0, n, CHUNK):
                at = slice(i * n + start, i * n + start + CHUNK)
                for coord, table in ((0, tx), (1, ty)):
                    row = ref[coord, e, pl.ds(m, 1), start : start + CHUNK]
                    for cells, hi, lo in hat_split(row):
                        table[m, cells, at] = hi
                        table[m, shifted(cells, GRID), at] = lo
        for coord in range(2):
            kept_ref[i, coord] = ref[coord, e]
    for m in range(2):
        out_ref[m] = table_product(tx.at[m], ty.at[m])
    row = lax.broadcasted_iota(jnp.int32, (PAD, PAD), 0)
    col = lax.broadcasted_iota(jnp.int32, (PAD, PAD), 1)
    flip = jnp.where(((row + col) & (PAD - 1)) == 0, 1.0, 0.0).astype(BF)
    copies[1].wait()
    for comp in range(2):
        for part in range(2):
            whole = kernel_ref[comp, part]
            hi, lo = hilo(whole)
            both = jnp.concatenate([dot(flip[:HALF], hi), dot(flip[:HALF], lo)], 0)
            both = dot(both.astype(BF), flip)
            turned = both[:HALF] + both[HALF:]
            if part == 0:
                half_ref[comp, part] = 0.5 * (whole[:HALF] + turned)
            else:
                half_ref[comp, part] = 0.5 * (whole[:HALF] - turned)
    for copy in copies[2:]:
        copy.wait()
    b = lax.axis_index("bunch")
    ndev = lax.axis_size("bunch")
    live = counts_ref[h, c]
    for s in range(partners_ref.shape[-1]):
        p = partners_ref[h, c, s]
        rel = lax.rem(lax.div(p, 2) - b + HOPS + 2 * ndev, ndev)
        r0 = offsets_ref[0, h, c, s] + OFFSET
        c0 = offsets_ref[1, h, c, s] + OFFSET
        used = jnp.where(s < live, 1, 0)
        code = ((used * 16 + rel * 2 + lax.rem(p, 2)) * 128 + r0) * 128 + c0
        slots_ref[s : s + 1, :] = jnp.full((1, 128), code, jnp.int32)


def first_deposit(positions, pos_c, kernel_hat, partners, offsets, counts):
    n = positions.shape[-1]
    small = (partners, offsets, counts)
    tables = [jnp.asarray(t) for t in dft_tables()]
    return pl.pallas_call(
        first_body,
        out_shape=[
            jax.ShapeDtypeStruct((2, GRID, GRID), F32),
            jax.ShapeDtypeStruct((2, 2, 2, n), F32),
            jax.ShapeDtypeStruct(positions.shape, F32),
            jax.ShapeDtypeStruct((2, 2, HALF, PAD), F32),
            jax.ShapeDtypeStruct((partners.shape[-1], 128), jnp.int32),
            *[jax.ShapeDtypeStruct(t.shape, BF) for t in tables],
        ],
        in_specs=[VM] + [HBM] * 9,
        out_specs=[VM] * 9,
        scratch_shapes=[
            *[pltpu.VMEM((2, 2 * GRID, 2 * n), BF)] * 2,
            pltpu.VMEM(kernel_hat.shape, F32),
            *[pltpu.SMEM(t.shape, jnp.int32) for t in small],
            pltpu.SemaphoreType.DMA((9,)),
        ],
        compiler_params=params(16),
        name="first_deposit",
    )(pos_c, *[in_hbm(t) for t in (positions, kernel_hat, *small, *tables)])


def kick_tables(ref, start, lanes, wx_ref, wy_ref, to):
    h = chip_half()
    c = core()
    rows = []
    for coord in range(2):
        both = ref[coord, h, :, start : start + lanes]
        rows.append(jnp.where(c == 0, both[0:1], both[1:2]))
    at = slice(to, to + lanes)
    wx_ref[:, at] = hat(rows[0], lanes)
    for cells, hi, lo in hat_split(rows[1]):
        wy_ref[cells, at] = hi
        wy_ref[shifted(cells, GRID), at] = hi
        wy_ref[shifted(cells, 2 * GRID), at] = lo


def kick_of(maps, wx, wy):
    t = dot(maps, wy)
    kx = jnp.sum(t[:GRID] * wx, axis=0, keepdims=True)
    ky = jnp.sum(t[GRID:] * wx, axis=0, keepdims=True)
    return kx, ky


def field_body(
    own_ref, r1_ref, r2_ref, s1_ref, s2_ref,
    half_ref, slots_ref, rows_ref, cols_ref, bcols_ref, brows_ref, wx_ref, wy_ref,
    maps_ref, out_ref,
    grids, source,
):
    c = core()
    slots = slots_ref[...]
    n = out_ref.shape[-1]
    places = (2, 1 + 2 * c, 4 * c, 3 - 2 * c, 4 - 4 * c)
    for ref, place in zip((own_ref, r1_ref, r2_ref, s1_ref, s2_ref), places):
        grids[2 * place] = ref[0]
        grids[2 * place + 1] = ref[1]
    source[...] = jnp.zeros_like(source)
    lane = lax.broadcasted_iota(jnp.int32, (GRID, GRID), 1)
    for s in range(slots_ref.shape[0]):
        code = slots[s, 0]
        c0 = code & 127
        r0 = lax.shift_right_logical(code, 7) & 127
        which = lax.shift_right_logical(code, 14) & 15
        gain = lax.shift_right_logical(code, 18).astype(F32)
        turned = pltpu.roll(grids[which], c0, 1) * gain
        low = jnp.where(lane >= c0, turned, 0.0)
        source[0, pl.ds(r0, GRID), :] += low
        source[1, pl.ds(r0, GRID), :] += turned - low
    hi, lo = hilo(jnp.concatenate([source[0, 0:SPAN, :], source[1, 0:SPAN, :]], 1))
    half = dot(rows_ref[...], jnp.concatenate([hi, lo, hi], 0))
    hi, lo = hilo(half)
    spec = dot(jnp.concatenate([hi, lo, hi], 1), cols_ref[...])
    spec_r = spec[:HALF, :PAD] + spec[HALF:, PAD:]
    spec_i = spec[HALF:, :PAD] - spec[:HALF, PAD:]
    back = []
    for comp in range(2):
        kr = half_ref[comp, 0]
        ki = half_ref[comp, 1]
        prod = jnp.concatenate([kr * spec_r - ki * spec_i, kr * spec_i + ki * spec_r], 0)
        hi, lo = hilo(prod)
        t = dot(jnp.concatenate([hi, lo, hi], 1), bcols_ref[...])
        re = t[:HALF, :GRID] - t[HALF:, GRID:]
        im = t[:GRID, GRID:] + t[HALF : HALF + GRID, :GRID]
        first = lax.broadcasted_iota(jnp.int32, (GRID, GRID), 0) == 0
        im = jnp.where(first, re[GRID : GRID + 1], im)
        back.append(jnp.concatenate([re[:GRID], im], 0))
    hi, lo = hilo(jnp.concatenate(back, 1))
    field = dot(brows_ref[...], jnp.concatenate([hi, lo, hi], 0))
    field = jnp.concatenate([field[:, :GRID], field[:, GRID:]], 0)
    hi, lo = hilo(field)
    maps = jnp.concatenate([hi, lo, hi], 1)
    maps_ref[...] = maps
    for start in range(0, n, CHUNK):
        at = slice(start, start + CHUNK)
        kx, ky = kick_of(maps, wx_ref[:, at], wy_ref[:, at])
        out_ref[0:1, start : start + CHUNK] = kx
        out_ref[1:2, start : start + CHUNK] = ky


def tables_body(pos_ref, wx_ref, wy_ref):
    for start in range(0, pos_ref.shape[-1], CHUNK):
        kick_tables(pos_ref, start, CHUNK, wx_ref, wy_ref, start)


def weight_tables(pos):
    n = pos.shape[-1]
    return pl.pallas_call(
        tables_body,
        out_shape=[jax.ShapeDtypeStruct((GRID, n), F32), jax.ShapeDtypeStruct((3 * GRID, n), BF)],
        in_specs=[VM],
        out_specs=[VM] * 2,
        compiler_params=params(8),
        name="weight_tables",
    )(pos)


def field(grids, half, slots, tables, weights):
    n = weights[0].shape[-1]
    return pl.pallas_call(
        field_body,
        out_shape=[
            jax.ShapeDtypeStruct((2 * GRID, 3 * GRID), BF),
            jax.ShapeDtypeStruct((2, n), F32),
        ],
        in_specs=[VM] * 13,
        out_specs=[VM] * 2,
        scratch_shapes=[
            pltpu.VMEM((4 * HOPS + 2, GRID, GRID), F32),
            pltpu.VMEM((2, SPAN + 8, GRID), F32),
        ],
        compiler_params=params(24),
        name="field",
    )(*grids, half, slots, *tables, *weights)


def kick_body(maps_ref, pa_ref, pc_ref, py_ref, near_ref, far_ref, wx_ref, wy_ref):
    maps = maps_ref[...]
    n = far_ref.shape[-1]
    for i, ref in enumerate((pa_ref, pc_ref, py_ref)):
        for start in range(0, n, CHUNK):
            at = slice(i * n + start, i * n + start + CHUNK)
            kick_tables(ref, start, CHUNK, wx_ref, wy_ref, i * n + start)
            kx, ky = kick_of(maps, wx_ref[:, at], wy_ref[:, at])
            to = slice(start, start + CHUNK)
            if i < 2:
                near_ref[i, 0:1, to] = kx
                near_ref[i, 1:2, to] = ky
            else:
                far_ref[0:1, to] = kx
                far_ref[1:2, to] = ky


def kick(maps, places):
    n = places[0].shape[-1]
    return pl.pallas_call(
        kick_body,
        out_shape=[jax.ShapeDtypeStruct((2, 2, n), F32), jax.ShapeDtypeStruct((2, n), F32)],
        in_specs=[VM] * 4,
        out_specs=[VM] * 2,
        scratch_shapes=[pltpu.VMEM((GRID, 3 * n), F32), pltpu.VMEM((3 * GRID, 3 * n), BF)],
        compiler_params=params(8),
        name="kick",
    )(maps, *places)


def finish_body(mine_ref, core_ref, chip_ref, momenta_ref, out_ref):
    h = chip_half()
    c = core()
    for coord in range(2):
        at = slice(coord, coord + 1)
        near = mine_ref[0, at, :]
        nearc = core_ref[1, at, :]
        far = chip_ref[0, at, :]
        farc = chip_ref[1, at, :]
        for beam in range(2):
            same = jnp.where(h == beam, near, far)
            other = jnp.where(h == beam, nearc, farc)
            both = jnp.concatenate(
                [jnp.where(c == 0, same, other), jnp.where(c == 0, other, same)], 0
            )
            out_ref[coord, beam] = momenta_ref[coord, beam] + both


def finish(mine, from_core, from_chip, momenta):
    return pl.pallas_call(
        finish_body,
        out_shape=jax.ShapeDtypeStruct(momenta.shape, F32),
        in_specs=[VM] * 4,
        out_specs=VM,
        compiler_params=params(4),
        name="finish",
    )(mine, from_core, from_chip, momenta)


def per_device(positions, momenta, kernel_hat, partners, offsets, counts):
    blocks = lax.axis_size("bunch")
    doms = lax.axis_size("dom")

    def across_cores(x):
        return lax.ppermute(x, "dom", [(i, i ^ 1) for i in range(doms)])

    def across_chips(x):
        return lax.ppermute(x, "dom", [(i, i ^ 2) for i in range(doms)])

    def along_blocks(x, by):
        pairs = []
        for i in range(blocks):
            for j in range(doms):
                to = (i + (by if j % 2 == 0 else -by)) % blocks
                pairs.append((i * doms + j, to * doms + j))
        return lax.ppermute(x, ("bunch", "dom"), pairs)

    pos_y = across_chips(positions)
    pos_c = across_cores(positions)
    first, near, pos_own, half, slots, *tables = first_deposit(
        positions, pos_c, kernel_hat, partners, offsets, counts
    )
    pos_y, first = lax.optimization_barrier((pos_y, first))
    pos_yc = across_cores(pos_y)
    second, kept_y = deposit([pos_y], first)
    message = pack(near, kept_y, pos_yc)
    p2 = along_blocks(message, 2)
    (own,) = deposit([pos_yc], second, False)
    r1 = along_blocks(own, 1)
    r2 = deposit_packed(p2)
    r1, r2 = lax.optimization_barrier((r1, r2))
    s2 = across_cores(r2)
    s1 = across_cores(r1)
    late_yc, r2 = lax.optimization_barrier((pos_yc, r2))
    weights = weight_tables(late_yc)
    maps, diagonal = field((own, r1, r2, s1, s2), half, slots, tables, weights)
    from_core_far = across_cores(diagonal)
    near, far = kick(maps, (pos_own, pos_c, pos_y))
    message, mine = lax.optimization_barrier((jnp.stack([far, from_core_far]), near))
    from_chip = across_chips(message)
    from_core = across_cores(mine)
    return finish(mine, from_core, from_chip, momenta)


def solution(mesh):
    in_specs = (
        P(None, None, "bunch", "dom"),
        P(None, None, "bunch", "dom"),
        P(),
        P(None, "bunch", None),
        P(None, None, "bunch", None),
        P(None, "bunch"),
    )
    out_specs = P(None, None, "bunch", "dom")
    return jax.shard_map(
        per_device, mesh=mesh, in_specs=in_specs, out_specs=out_specs, check_vma=False
    )
```

```python
import functools

import jax
import jax.numpy as jnp
import numpy as np
from jax import lax
from jax.experimental import pallas as pl
from jax.experimental.pallas import tpu as pltpu
from jax.sharding import PartitionSpec as P

GRID = 128
PAD = 256
OFFSET = 32
SPAN = GRID + 2 * OFFSET
HALF = 136
HOPS = 2
CHUNK = 512
TILE = 16
DEP_US = 0.01
PACKED_US = 100.0
BF = jnp.bfloat16
F32 = jnp.float32
VM = pl.BlockSpec(memory_space=pltpu.VMEM)
SM = pl.BlockSpec(memory_space=pltpu.SMEM)
HBM = pl.BlockSpec(memory_space=pltpu.HBM)


def in_hbm(x):
    return pltpu.with_memory_space_constraint(x, pltpu.HBM)


def split_const(m):
    hi = m.astype(BF)
    lo = (m - hi.astype(np.float64)).astype(BF)
    return np.asarray(hi), np.asarray(lo)


def dft_tables():
    k = np.arange(PAD)
    w = 2.0 * np.pi / PAD
    half = np.arange(HALF)
    used = (half <= GRID)[:, None]
    r = np.arange(SPAN) - OFFSET
    ang = w * ((half[:, None] * r[None, :]) % PAD)
    hi, lo = split_const(np.concatenate([np.cos(ang) * used, -np.sin(ang) * used], 0))
    rows = np.concatenate([hi, hi, lo], 1)
    r = np.arange(PAD) - OFFSET
    ang = w * ((r[:, None] * k[None, :]) % PAD)
    hi, lo = split_const(np.concatenate([np.cos(ang), np.sin(ang)], 1))
    cols = np.concatenate([hi, hi, lo], 0)
    j = np.arange(GRID)
    ang = w * ((k[:, None] * j[None, :]) % PAD)
    hi, lo = split_const(np.concatenate([np.cos(ang), np.sin(ang)], 1))
    back_cols = np.concatenate([hi, hi, lo], 0)
    ang = w * ((j[:, None] * np.arange(GRID)[None, :]) % PAD)
    re = 2.0 * np.cos(ang)
    re[:, 0] = 1.0
    im = -2.0 * np.sin(ang)
    im[:, 0] = np.cos(np.pi * j)
    hi, lo = split_const(np.concatenate([re, im], 1) / (PAD * PAD))
    back_rows = np.concatenate([hi, hi, lo], 1)
    return rows, cols, back_cols, back_rows


def hilo(v):
    hi = v.astype(BF)
    lo = (v - hi.astype(F32)).astype(BF)
    return hi, lo


def dot(a, b):
    return jnp.dot(a, b, preferred_element_type=F32)


def hat(coord, lanes):
    cells = lax.broadcasted_iota(jnp.int32, (GRID, lanes), 0).astype(F32)
    return jnp.maximum(0.0, 1.0 - jnp.abs(coord - cells))


def hat_split(coord):
    lanes = coord.shape[-1]
    cell = jnp.floor(coord)
    frac = coord - cell
    coarse = jnp.floor(frac * 256.0) * (1.0 / 256.0)
    fine = frac - coarse

    def rows(v):
        return jnp.broadcast_to(v, (TILE, lanes)).astype(BF)

    here, there = rows(cell), rows(cell + 1.0)
    hi = (rows(1.0 - coarse), rows(coarse))
    lo = (rows(-fine), rows(fine))
    zero = jnp.zeros((TILE, lanes), BF)
    base = lax.broadcasted_iota(jnp.int32, (TILE, lanes), 0).astype(F32)
    for start in range(0, GRID, TILE):
        cells = (base + float(start)).astype(BF)
        at_here = cells == here
        at_there = cells == there
        yield (
            slice(start, start + TILE),
            jnp.where(at_here, hi[0], jnp.where(at_there, hi[1], zero)),
            jnp.where(at_here, lo[0], jnp.where(at_there, lo[1], zero)),
        )


def shifted(rows, by):
    return slice(rows.start + by, rows.stop + by)


def chip_half():
    return lax.div(lax.axis_index("dom"), 2)


def core():
    return lax.rem(lax.axis_index("dom"), 2)


def cost(us):
    return pl.CostEstimate(flops=int(us * 1e9), transcendentals=0, bytes_accessed=0)


def params(mib):
    return pltpu.CompilerParams(vmem_limit_bytes=mib * 1024 * 1024)


def deposit_rows(rows, tx, ty):
    for start, coords in rows:
        for coord, table in zip(coords, (tx, ty)):
            n = coord.shape[-1]
            at = slice(start, start + n)
            for cells, hi, lo in hat_split(coord):
                table[cells, at] = hi
                table[shifted(cells, GRID), at] = lo
    return table_product(tx, ty)


def table_product(tx, ty):
    acc = lax.dot_general(
        tx[...], ty[...], (((1,), (1,)), ((), ())), preferred_element_type=F32
    )
    return (acc[:GRID, :GRID] + acc[GRID:, GRID:]) + (acc[:GRID, GRID:] + acc[GRID:, :GRID])


def deposit_body(sources, keep, *refs):
    given = refs[: len(refs) - (4 if keep else 3)]
    out_ref, *kept, tx, ty = refs[len(given) :]
    prev_ref = given[sources] if len(given) > sources else None
    e = 1 - chip_half()
    n = given[0].shape[-1]
    for m in range(2):
        rows = []
        for i, ref in enumerate(given[:sources]):
            for start in range(0, n, CHUNK):
                at = slice(start, start + CHUNK)
                rows.append(
                    (i * n + start, [ref[coord, e, pl.ds(m, 1), at] for coord in range(2)])
                )
        total = deposit_rows(rows, tx.at[m], ty.at[m])
        if prev_ref is not None:
            total = total + prev_ref[m]
        out_ref[m] = total
    for kept_ref in kept:
        for i, ref in enumerate(given[:sources]):
            for coord in range(2):
                kept_ref[i, coord] = ref[coord, e]


def deposit(sources, prev=None, keep=True):
    n = sources[0].shape[-1]
    args = [*sources] + ([] if prev is None else [prev])
    return pl.pallas_call(
        functools.partial(deposit_body, len(sources), keep),
        out_shape=[
            jax.ShapeDtypeStruct((2, GRID, GRID), F32),
            jax.ShapeDtypeStruct((len(sources), 2, 2, n), F32),
        ][: 1 + keep],
        in_specs=[VM] * len(args),
        out_specs=[VM] * (1 + keep),
        scratch_shapes=[pltpu.VMEM((2, 2 * GRID, len(sources) * n), BF)] * 2,
        compiler_params=params(16),
        cost_estimate=cost(DEP_US),
        name="deposit",
    )(*args)


def pack_body(near_ref, y_ref, yc_ref, out_ref):
    e = 1 - chip_half()
    out_ref[0] = near_ref[0]
    out_ref[1] = near_ref[1]
    out_ref[2] = y_ref[0]
    for coord in range(2):
        out_ref[3, coord] = yc_ref[coord, e]


def pack(near, y, yc):
    return pl.pallas_call(
        pack_body,
        out_shape=jax.ShapeDtypeStruct((4, *near.shape[1:]), F32),
        in_specs=[VM] * 3,
        out_specs=VM,
        compiler_params=params(4),
        name="pack",
    )(near, y, yc)


def deposit_packed_body(pos_ref, out_ref, tx, ty):
    sources, _, members, n = pos_ref.shape
    for m in range(members):
        rows = []
        for i in range(sources):
            for start in range(0, n, CHUNK):
                at = slice(start, start + CHUNK)
                rows.append(
                    (i * n + start, [pos_ref[i, coord, m : m + 1, at] for coord in range(2)])
                )
        out_ref[m] = deposit_rows(rows, tx.at[m], ty.at[m])


def deposit_packed(pos):
    return pl.pallas_call(
        deposit_packed_body,
        out_shape=jax.ShapeDtypeStruct((2, GRID, GRID), F32),
        in_specs=[VM],
        out_specs=VM,
        scratch_shapes=[pltpu.VMEM((2, 2 * GRID, pos.shape[0] * pos.shape[-1]), BF)] * 2,
        compiler_params=params(20),
        cost_estimate=cost(PACKED_US),
        name="deposit_packed",
    )(pos)


def first_body(
    pc_ref, pa_hbm, kernel_hbm, partners_hbm, offsets_hbm, counts_hbm,
    rows_hbm, cols_hbm, bcols_hbm, brows_hbm,
    out_ref, kept_ref, pa_ref, half_ref, slots_ref, rows_ref, cols_ref, bcols_ref, brows_ref,
    tx, ty, kernel_ref, partners_ref, offsets_ref, counts_ref, sems,
):
    copies = [
        pltpu.make_async_copy(src, dst, sems.at[i])
        for i, (src, dst) in enumerate((
            (pa_hbm, pa_ref), (kernel_hbm, kernel_ref), (partners_hbm, partners_ref),
            (offsets_hbm, offsets_ref), (counts_hbm, counts_ref), (rows_hbm, rows_ref),
            (cols_hbm, cols_ref), (bcols_hbm, bcols_ref), (brows_hbm, brows_ref),
        ))
    ]
    for copy in copies:
        copy.start()
    h = chip_half()
    c = core()
    e = 1 - h
    n = pc_ref.shape[-1]
    for i, ref in ((1, pc_ref), (0, pa_ref)):
        if i == 0:
            copies[0].wait()
        for m in range(2):
            for start in range(0, n, CHUNK):
                at = slice(i * n + start, i * n + start + CHUNK)
                for coord, table in ((0, tx), (1, ty)):
                    row = ref[coord, e, pl.ds(m, 1), start : start + CHUNK]
                    for cells, hi, lo in hat_split(row):
                        table[m, cells, at] = hi
                        table[m, shifted(cells, GRID), at] = lo
        for coord in range(2):
            kept_ref[i, coord] = ref[coord, e]
    for m in range(2):
        out_ref[m] = table_product(tx.at[m], ty.at[m])
    row = lax.broadcasted_iota(jnp.int32, (PAD, PAD), 0)
    col = lax.broadcasted_iota(jnp.int32, (PAD, PAD), 1)
    flip = jnp.where(((row + col) & (PAD - 1)) == 0, 1.0, 0.0).astype(BF)
    copies[1].wait()
    for comp in range(2):
        for part in range(2):
            whole = kernel_ref[comp, part]
            hi, lo = hilo(whole)
            both = jnp.concatenate([dot(flip[:HALF], hi), dot(flip[:HALF], lo)], 0)
            both = dot(both.astype(BF), flip)
            turned = both[:HALF] + both[HALF:]
            if part == 0:
                half_ref[comp, part] = 0.5 * (whole[:HALF] + turned)
            else:
                half_ref[comp, part] = 0.5 * (whole[:HALF] - turned)
    for copy in copies[2:]:
        copy.wait()
    b = lax.axis_index("bunch")
    ndev = lax.axis_size("bunch")
    live = counts_ref[h, c]
    for s in range(partners_ref.shape[-1]):
        p = partners_ref[h, c, s]
        rel = lax.rem(lax.div(p, 2) - b + HOPS + 2 * ndev, ndev)
        r0 = offsets_ref[0, h, c, s] + OFFSET
        c0 = offsets_ref[1, h, c, s] + OFFSET
        used = jnp.where(s < live, 1, 0)
        code = ((used * 16 + rel * 2 + lax.rem(p, 2)) * 128 + r0) * 128 + c0
        slots_ref[s : s + 1, :] = jnp.full((1, 128), code, jnp.int32)


def first_deposit(positions, pos_c, kernel_hat, partners, offsets, counts):
    n = positions.shape[-1]
    small = (partners, offsets, counts)
    tables = [jnp.asarray(t) for t in dft_tables()]
    return pl.pallas_call(
        first_body,
        out_shape=[
            jax.ShapeDtypeStruct((2, GRID, GRID), F32),
            jax.ShapeDtypeStruct((2, 2, 2, n), F32),
            jax.ShapeDtypeStruct(positions.shape, F32),
            jax.ShapeDtypeStruct((2, 2, HALF, PAD), F32),
            jax.ShapeDtypeStruct((partners.shape[-1], 128), jnp.int32),
            *[jax.ShapeDtypeStruct(t.shape, BF) for t in tables],
        ],
        in_specs=[VM] + [HBM] * 9,
        out_specs=[VM] * 9,
        scratch_shapes=[
            *[pltpu.VMEM((2, 2 * GRID, 2 * n), BF)] * 2,
            pltpu.VMEM(kernel_hat.shape, F32),
            *[pltpu.SMEM(t.shape, jnp.int32) for t in small],
            pltpu.SemaphoreType.DMA((9,)),
        ],
        compiler_params=params(16),
        name="first_deposit",
    )(pos_c, *[in_hbm(t) for t in (positions, kernel_hat, *small, *tables)])


def kick_tables(ref, start, lanes, wx_ref, wy_ref, to):
    h = chip_half()
    c = core()
    rows = []
    for coord in range(2):
        both = ref[coord, h, :, start : start + lanes]
        rows.append(jnp.where(c == 0, both[0:1], both[1:2]))
    at = slice(to, to + lanes)
    wx_ref[:, at] = hat(rows[0], lanes)
    for cells, hi, lo in hat_split(rows[1]):
        wy_ref[cells, at] = hi
        wy_ref[shifted(cells, GRID), at] = hi
        wy_ref[shifted(cells, 2 * GRID), at] = lo


def kick_of(maps, wx, wy):
    t = dot(maps, wy)
    kx = jnp.sum(t[:GRID] * wx, axis=0, keepdims=True)
    ky = jnp.sum(t[GRID:] * wx, axis=0, keepdims=True)
    return kx, ky


def field_body(
    own_ref, r1_ref, r2_ref, both_ref,
    half_ref, slots_ref, rows_ref, cols_ref, bcols_ref, brows_ref, pyc_ref,
    maps_ref, out_ref,
    wx_ref, wy_ref, grids, source,
):
    c = core()
    slots = slots_ref[...]
    n = out_ref.shape[-1]
    for start in range(0, n, CHUNK):
        kick_tables(pyc_ref, start, CHUNK, wx_ref, wy_ref, start)
    places = (2, 1 + 2 * c, 4 * c, 3 - 2 * c, 4 - 4 * c)
    for ref, place in zip((own_ref, r1_ref, r2_ref), places):
        grids[2 * place] = ref[0]
        grids[2 * place + 1] = ref[1]
    for i, place in enumerate(places[3:]):
        grids[2 * place] = both_ref[2 * i]
        grids[2 * place + 1] = both_ref[2 * i + 1]
    source[...] = jnp.zeros_like(source)
    lane = lax.broadcasted_iota(jnp.int32, (GRID, GRID), 1)
    for s in range(slots_ref.shape[0]):
        code = slots[s, 0]
        c0 = code & 127
        r0 = lax.shift_right_logical(code, 7) & 127
        which = lax.shift_right_logical(code, 14) & 15
        gain = lax.shift_right_logical(code, 18).astype(F32)
        turned = pltpu.roll(grids[which], c0, 1) * gain
        low = jnp.where(lane >= c0, turned, 0.0)
        source[0, pl.ds(r0, GRID), :] += low
        source[1, pl.ds(r0, GRID), :] += turned - low
    hi, lo = hilo(jnp.concatenate([source[0, 0:SPAN, :], source[1, 0:SPAN, :]], 1))
    half = dot(rows_ref[...], jnp.concatenate([hi, lo, hi], 0))
    hi, lo = hilo(half)
    spec = dot(jnp.concatenate([hi, lo, hi], 1), cols_ref[...])
    spec_r = spec[:HALF, :PAD] + spec[HALF:, PAD:]
    spec_i = spec[HALF:, :PAD] - spec[:HALF, PAD:]
    back = []
    for comp in range(2):
        kr = half_ref[comp, 0]
        ki = half_ref[comp, 1]
        prod = jnp.concatenate([kr * spec_r - ki * spec_i, kr * spec_i + ki * spec_r], 0)
        hi, lo = hilo(prod)
        t = dot(jnp.concatenate([hi, lo, hi], 1), bcols_ref[...])
        re = t[:HALF, :GRID] - t[HALF:, GRID:]
        im = t[:GRID, GRID:] + t[HALF : HALF + GRID, :GRID]
        first = lax.broadcasted_iota(jnp.int32, (GRID, GRID), 0) == 0
        im = jnp.where(first, re[GRID : GRID + 1], im)
        back.append(jnp.concatenate([re[:GRID], im], 0))
    hi, lo = hilo(jnp.concatenate(back, 1))
    field = dot(brows_ref[...], jnp.concatenate([hi, lo, hi], 0))
    field = jnp.concatenate([field[:, :GRID], field[:, GRID:]], 0)
    hi, lo = hilo(field)
    maps = jnp.concatenate([hi, lo, hi], 1)
    maps_ref[...] = maps
    for start in range(0, n, CHUNK):
        at = slice(start, start + CHUNK)
        kx, ky = kick_of(maps, wx_ref[:, at], wy_ref[:, at])
        out_ref[0:1, start : start + CHUNK] = kx
        out_ref[1:2, start : start + CHUNK] = ky


def field(grids, half, slots, tables, pos_yc):
    n = pos_yc.shape[-1]
    return pl.pallas_call(
        field_body,
        out_shape=[
            jax.ShapeDtypeStruct((2 * GRID, 3 * GRID), BF),
            jax.ShapeDtypeStruct((2, n), F32),
        ],
        in_specs=[VM] * 11,
        out_specs=[VM] * 2,
        scratch_shapes=[
            pltpu.VMEM((GRID, n), F32),
            pltpu.VMEM((3 * GRID, n), BF),
            pltpu.VMEM((4 * HOPS + 2, GRID, GRID), F32),
            pltpu.VMEM((2, SPAN + 8, GRID), F32),
        ],
        compiler_params=params(24),
        name="field",
    )(*grids, half, slots, *tables, pos_yc)


def kick_body(maps_ref, pa_ref, pc_ref, py_ref, near_ref, far_ref, wx_ref, wy_ref):
    maps = maps_ref[...]
    n = far_ref.shape[-1]
    for i, ref in enumerate((pa_ref, pc_ref, py_ref)):
        for start in range(0, n, CHUNK):
            at = slice(i * n + start, i * n + start + CHUNK)
            kick_tables(ref, start, CHUNK, wx_ref, wy_ref, i * n + start)
            kx, ky = kick_of(maps, wx_ref[:, at], wy_ref[:, at])
            to = slice(start, start + CHUNK)
            if i < 2:
                near_ref[i, 0:1, to] = kx
                near_ref[i, 1:2, to] = ky
            else:
                far_ref[0:1, to] = kx
                far_ref[1:2, to] = ky


def kick(maps, places):
    n = places[0].shape[-1]
    return pl.pallas_call(
        kick_body,
        out_shape=[jax.ShapeDtypeStruct((2, 2, n), F32), jax.ShapeDtypeStruct((2, n), F32)],
        in_specs=[VM] * 4,
        out_specs=[VM] * 2,
        scratch_shapes=[pltpu.VMEM((GRID, 3 * n), F32), pltpu.VMEM((3 * GRID, 3 * n), BF)],
        compiler_params=params(8),
        name="kick",
    )(maps, *places)


def finish_body(mine_ref, core_ref, chip_ref, momenta_ref, out_ref):
    h = chip_half()
    c = core()
    for coord in range(2):
        at = slice(coord, coord + 1)
        near = mine_ref[0, at, :]
        nearc = core_ref[1, at, :]
        far = chip_ref[0, at, :]
        farc = chip_ref[1, at, :]
        for beam in range(2):
            same = jnp.where(h == beam, near, far)
            other = jnp.where(h == beam, nearc, farc)
            both = jnp.concatenate(
                [jnp.where(c == 0, same, other), jnp.where(c == 0, other, same)], 0
            )
            out_ref[coord, beam] = momenta_ref[coord, beam] + both


def finish(mine, from_core, from_chip, momenta):
    return pl.pallas_call(
        finish_body,
        out_shape=jax.ShapeDtypeStruct(momenta.shape, F32),
        in_specs=[VM] * 4,
        out_specs=VM,
        compiler_params=params(4),
        name="finish",
    )(mine, from_core, from_chip, momenta)


def per_device(positions, momenta, kernel_hat, partners, offsets, counts):
    blocks = lax.axis_size("bunch")
    doms = lax.axis_size("dom")

    def across_cores(x):
        return lax.ppermute(x, "dom", [(i, i ^ 1) for i in range(doms)])

    def across_chips(x):
        return lax.ppermute(x, "dom", [(i, i ^ 2) for i in range(doms)])

    def along_blocks(x, by):
        pairs = []
        for i in range(blocks):
            for j in range(doms):
                to = (i + (by if j % 2 == 0 else -by)) % blocks
                pairs.append((i * doms + j, to * doms + j))
        return lax.ppermute(x, ("bunch", "dom"), pairs)

    pos_y = across_chips(positions)
    pos_c = across_cores(positions)
    first, near, pos_own, half, slots, *tables = first_deposit(
        positions, pos_c, kernel_hat, partners, offsets, counts
    )
    pos_y, first = lax.optimization_barrier((pos_y, first))
    pos_yc = across_cores(pos_y)
    second, kept_y = deposit([pos_y], first)
    message = pack(near, kept_y, pos_yc)
    p2 = along_blocks(message, 2)
    (own,) = deposit([pos_yc], second, False)
    r1 = along_blocks(own, 1)
    r2 = deposit_packed(p2)
    r1, r2 = lax.optimization_barrier((r1, r2))
    both = across_cores(jnp.concatenate([r1, r2], 0))
    maps, diagonal = field((own, r1, r2, both), half, slots, tables, pos_yc)
    from_core_far = across_cores(diagonal)
    near, far = kick(maps, (pos_own, pos_c, pos_y))
    message, mine = lax.optimization_barrier((jnp.stack([far, from_core_far]), near))
    from_chip = across_chips(message)
    from_core = across_cores(mine)
    return finish(mine, from_core, from_chip, momenta)


def solution(mesh):
    in_specs = (
        P(None, None, "bunch", "dom"),
        P(None, None, "bunch", "dom"),
        P(),
        P(None, "bunch", None),
        P(None, None, "bunch", None),
        P(None, "bunch"),
    )
    out_specs = P(None, None, "bunch", "dom")
    return jax.shard_map(
        per_device, mesh=mesh, in_specs=in_specs, out_specs=out_specs, check_vma=False
    )
```
